1024 devices in a mesh: ctx: 64 (over z, core), tp: 16 (over y, x).
Axes of the slice: x: 4, y: 4, z: 32, core: 2. Of those that a mesh axis runs over, the one named last changes fastest.
Arguments:
- x_in: bfloat16 [8192, 16384], P('ctx', 'tp'), may hold values from -6 to 6
- z_in: bfloat16 [8192, 16384], P('ctx', 'tp'), may hold values from -6 to 6
- b_in: bfloat16 [8192, 2048], P('ctx', 'tp'), may hold values from -6 to 6
- c_in: bfloat16 [8192, 2048], P('ctx', 'tp'), may hold values from -6 to 6
- dt_raw: float32 [8192, 256], P('ctx', 'tp'), may hold values from -2 to 2
- dt_bias: float32 [256], P('tp'), may hold values from -5.8 to -4.2
- a_log: float32 [256], P('tp'), may hold values from -2 to 1.1
- d_skip: float32 [256], P('tp'), may hold values from 0.5 to 1.5
- conv_x: float32 [4, 16384], P(None, 'tp'), may hold values from -3 to 3
- conv_b: float32 [4, 2048], P(None, 'tp'), may hold values from -3 to 3
- conv_c: float32 [4, 2048], P(None, 'tp'), may hold values from -3 to 3
- norm_gain: float32 [16384], P('tp'), may hold values from 0.1 to 1.9
Outputs:
- mixed_out: bfloat16 [16384, 8192], P(('tp', 'ctx'))
The draws below stay inside these ranges and needn't reach their ends.
All inputs are finite; a program needn't handle non-finite values.
Results may differ from the reference program's by a relative error of at most 0.007.
Values may be sent and summed in bfloat16 or wider, within the bound.
No kernel may reach another device: no remote copies, remote signals or barrier semaphores. Data moves between devices by JAX's collectives and lax.ppermute only.
A program may use at most 128 MiB of HBM per device.

```python
import jax
import jax.numpy as jnp
from jax import lax

HEADS = 256
HEAD_DIM = 64
STATE = 128
CONV = 4
SPAN = 128
TOK_DEV = 128
TOKENS = 8192
GROUPS = 16
HEADS_DEV = 16
CHANNELS = 16384


def head_kinds(key):
    share = 0.5
    return jax.random.uniform(jax.random.fold_in(key, 11), (HEADS,)) < share


def draw_a_log(key, part):
    slower = head_kinds(key)
    slow_values = jax.random.uniform(jax.random.fold_in(key, 12), (HEADS,), jnp.float32, -1.8, -0.4)
    fast_values = jax.random.uniform(jax.random.fold_in(key, 13), (HEADS,), jnp.float32, 0.3, 1.1)
    return jnp.where(slower, slow_values, fast_values)


def draw_dt_bias(key, part):
    slower = head_kinds(key)
    slow_values = jax.random.uniform(jax.random.fold_in(key, 14), (HEADS,), jnp.float32, -5.8, -5.2)
    fast_values = jax.random.uniform(jax.random.fold_in(key, 15), (HEADS,), jnp.float32, -4.6, -4.2)
    return jnp.where(slower, slow_values, fast_values)


def draw_dt_raw(key, part):
    offsets = jax.random.uniform(jax.random.fold_in(key, 21), (TOKENS // TOK_DEV, 1, HEADS), jnp.float32, -0.7, 0.7)
    noise = 0.5 * jnp.clip(jax.random.normal(jax.random.fold_in(key, 23), (TOKENS // TOK_DEV, TOK_DEV, HEADS), jnp.float32), -2.5, 2.5)
    return (offsets + noise).reshape(TOKENS, HEADS)


def level_of(key, dims, cuts, low, high):
    loudness = 1.0
    for position, parts in cuts:
        steps = jax.random.uniform(jax.random.fold_in(jax.random.fold_in(key, 6), position), (parts,), jnp.float32, low / len(cuts), high / len(cuts))
        loudness = loudness * jnp.repeat(jnp.exp(steps), dims[position] // parts).reshape((-1,) + (1,) * (len(dims) - 1 - position))
    return loudness


def gaussian(rng, extent, scale, bound, split=(), held_as=jnp.bfloat16):
    result = scale * jax.random.normal(rng, extent, jnp.float32)
    if split:
        result = result * level_of(rng, extent, split, -0.22, 0.18)
    return jnp.clip(result, -bound, bound).astype(held_as)


def setup_inputs(seed: int = 0) -> dict:
    splits = jax.random.split(jax.random.key(seed), 13)
    x_in = gaussian(splits[0], (TOKENS, CHANNELS), 1.0, 6.0, ((0, 64), (1, 16)))
    z_in = gaussian(splits[1], (TOKENS, CHANNELS), 1.0, 6.0, ((0, 64), (1, 16)))
    b_in = gaussian(splits[2], (TOKENS, GROUPS * STATE), 1.0, 6.0, ((0, 64), (1, 16)))
    c_in = gaussian(splits[3], (TOKENS, GROUPS * STATE), 1.0, 6.0, ((0, 64), (1, 16)))
    dt_raw = draw_dt_raw(jax.random.fold_in(splits[12], 71), 0)
    dt_bias = draw_dt_bias(jax.random.fold_in(splits[12], 71), 0)
    a_log = draw_a_log(jax.random.fold_in(splits[12], 71), 0)
    d_skip = jnp.clip(0.5 + 1.0 * jax.random.uniform(splits[7], (HEADS,), jnp.float32) ** level_of(splits[7], (HEADS,), ((0, 16),), -0.2, 0.2), 0.5, 1.5)
    conv_x = gaussian(splits[8], (CONV, CHANNELS), CONV ** -0.5, 3.0, ((1, 16),), jnp.float32)
    conv_b = gaussian(splits[9], (CONV, GROUPS * STATE), CONV ** -0.5, 3.0, ((1, 16),), jnp.float32)
    conv_c = gaussian(splits[10], (CONV, GROUPS * STATE), CONV ** -0.5, 3.0, ((1, 16),), jnp.float32)
    norm_gain = jnp.clip(1.0 + 0.18 * jax.random.normal(splits[11], (CHANNELS,), jnp.float32), 0.1, 1.9)
    return dict(x_in=x_in, z_in=z_in, b_in=b_in, c_in=c_in, dt_raw=dt_raw, dt_bias=dt_bias, a_log=a_log, d_skip=d_skip, conv_x=conv_x, conv_b=conv_b, conv_c=conv_c, norm_gain=norm_gain)


def causal_silu(padded, taps):
    rows_f = padded.astype(jnp.float32)
    total = taps[0] * rows_f[0:SPAN]
    for offset in range(1, CONV):
        total = total + taps[offset] * rows_f[offset:offset + SPAN]
    return jax.nn.silu(total).astype(jnp.bfloat16)

def rounded(value):
    return lax.optimization_barrier(value.astype(jnp.bfloat16)).astype(jnp.float32)

def reference(x_in, z_in, b_in, c_in, dt_raw, dt_bias, a_log, d_skip, conv_x, conv_b, conv_c, norm_gain):
    blocks = TOKENS // SPAN
    x_pad = jnp.pad(x_in, ((CONV - 1, 0), (0, 0)))
    b_pad = jnp.pad(b_in, ((CONV - 1, 0), (0, 0)))
    c_pad = jnp.pad(c_in, ((CONV - 1, 0), (0, 0)))
    decay_rate = jnp.exp(a_log)
    lower = jnp.tril(jnp.ones((SPAN, SPAN), dtype=bool))

    def block_step(state, index):
        start = (index * SPAN).astype(jnp.int32)
        x_act = causal_silu(lax.dynamic_slice_in_dim(x_pad, start, SPAN + CONV - 1, 0), conv_x)
        b_act = causal_silu(lax.dynamic_slice_in_dim(b_pad, start, SPAN + CONV - 1, 0), conv_b)
        c_act = causal_silu(lax.dynamic_slice_in_dim(c_pad, start, SPAN + CONV - 1, 0), conv_c)
        delta = jax.nn.softplus(lax.dynamic_slice_in_dim(dt_raw, start, SPAN, 0) + dt_bias)
        logs = jnp.cumsum(-decay_rate * delta, axis=0)
        heads_x = x_act.reshape(SPAN, HEADS, HEAD_DIM).astype(jnp.float32)
        group_b = b_act.reshape(SPAN, GROUPS, STATE).astype(jnp.float32)
        group_c = c_act.reshape(SPAN, GROUPS, STATE).astype(jnp.float32)
        scores = jnp.einsum('tgn,sgn->gts', group_c, group_b)
        scores = jnp.repeat(scores, HEADS_DEV, axis=0)
        logs_t = logs.T
        gap = jnp.where(lower[None], logs_t[:, :, None] - logs_t[:, None, :], 0.0)
        decay = jnp.where(lower[None], jnp.exp(gap), 0.0)
        weights = rounded(scores * decay * delta.T[:, None, :])
        inner = jnp.einsum('hts,shp->thp', weights, heads_x)
        state_low = rounded(state).reshape(GROUPS, HEADS_DEV, HEAD_DIM, STATE)
        outer = jnp.einsum('tgn,ghpn->tghp', group_c, state_low).reshape(SPAN, HEADS, HEAD_DIM)
        y_val = inner + jnp.exp(logs)[:, :, None] * outer + d_skip[None, :, None] * heads_x
        last = logs[-1]
        scaled = rounded((jnp.exp(last[None, :] - logs) * delta)[:, :, None] * heads_x)
        update = jnp.einsum('sghp,sgn->ghpn', scaled.reshape(SPAN, GROUPS, HEADS_DEV, HEAD_DIM), group_b)
        new_state = jnp.exp(last)[:, None, None] * state + update.reshape(HEADS, HEAD_DIM, STATE)
        z_rows = lax.dynamic_slice_in_dim(z_in, start, SPAN, 0).astype(jnp.float32)
        gated = (y_val.reshape(SPAN, CHANNELS) * jax.nn.silu(z_rows)).reshape(SPAN, GROUPS, HEADS_DEV * HEAD_DIM)
        meansq = lax.optimization_barrier(jnp.mean(gated * gated, axis=-1, keepdims=True))
        normed = (gated * lax.rsqrt(meansq + 1e-05)).reshape(SPAN, CHANNELS) * norm_gain
        return (new_state, normed.astype(jnp.bfloat16))
    start_state = jnp.zeros((HEADS, HEAD_DIM, STATE), jnp.float32)
    _, pieces = lax.scan(block_step, start_state, jnp.arange(blocks, dtype=jnp.int32))
    return pieces.reshape(TOKENS, CHANNELS).T
```

```python
import jax
import jax.numpy as jnp
from jax import lax
from jax.sharding import PartitionSpec as P

SPAN = 128
NEAR = 8


def causal_silu(padded, taps, length):
    rows_f = padded.astype(jnp.float32)
    total = taps[0] * rows_f[0:length]
    for offset in range(1, taps.shape[0]):
        total = total + taps[offset] * rows_f[offset : offset + length]
    return jax.nn.silu(total).astype(jnp.bfloat16)


def split3(value):
    first = lax.reduce_precision(value, 8, 7)
    rest = value - first
    second = lax.reduce_precision(rest, 8, 7)
    third = rest - second
    return [part.astype(jnp.bfloat16) for part in (first, second, third)]


def with_logs(body, logs):
    rows = jnp.concatenate(split3(logs), axis=-1)
    rows = jnp.pad(rows, [(0, 0)] * (rows.ndim - 1) + [(0, 16 - rows.shape[-1])])
    rows = jnp.broadcast_to(rows[..., None], rows.shape + (body.shape[-1],))
    return jnp.concatenate([body.astype(jnp.bfloat16), rows], axis=-2)


def read_logs(message):
    parts = message[..., 128:134, :].astype(jnp.float32)
    return parts[..., 0:2, :] + parts[..., 2:4, :] + parts[..., 4:6, :]


def widen(logs):
    return jnp.repeat(jnp.exp(logs), 64, axis=-2)


def entering_states(update, last):
    count = lax.axis_size("ctx")
    groups = count // NEAR
    near = [list(range(g * NEAR, (g + 1) * NEAR)) for g in range(groups)]
    far = [[i + NEAR * g for g in range(groups)] for i in range(NEAR)]
    mine = lax.axis_index("ctx") // NEAR
    message = with_logs(update.reshape(NEAR, 128, 128), last.reshape(NEAR, 2))
    message = lax.all_to_all(message, "ctx", 0, 0, tiled=True, axis_index_groups=near)
    parts = message[:, :128].astype(jnp.float32)
    part_logs = read_logs(message)
    inside, inside_logs = [jnp.zeros((128, 128), jnp.float32)], [jnp.zeros((2, 128), jnp.float32)]
    for k in range(NEAR):
        inside.append(widen(part_logs[k]) * inside[-1] + parts[k])
        inside_logs.append(inside_logs[-1] + part_logs[k])
    totals = lax.all_gather(
        with_logs(inside[NEAR], inside_logs[NEAR][:, 0]), "ctx", axis_index_groups=far
    )
    before = jnp.zeros((128, 128), jnp.float32)
    total_logs = read_logs(totals)
    for g in range(groups - 1):
        new = widen(total_logs[g]) * before + totals[g, :128].astype(jnp.float32)
        before = jnp.where(g < mine, new, before)
    states = jnp.stack(
        [(inside[k] + widen(inside_logs[k]) * before).astype(jnp.bfloat16) for k in range(NEAR)]
    )
    states = lax.all_to_all(states, "ctx", 0, 0, tiled=True, axis_index_groups=near)
    return states.reshape(update.shape)


def shards(
    x_in, z_in, b_in, c_in, dt_raw, dt_bias, a_log, d_skip, conv_x, conv_b, conv_c, norm_gain
):
    length, width = x_in.shape
    heads = dt_raw.shape[1]
    head_size = width // heads
    state = b_in.shape[1]
    taps = conv_x.shape[0]
    count = lax.axis_size("ctx")
    tails = jnp.concatenate([v[length - taps + 1 :] for v in (x_in, b_in, c_in)], axis=1)
    tails = lax.ppermute(tails, "ctx", [(i, i + 1) for i in range(count - 1)])
    tail_x, tail_b, tail_c = jnp.split(tails, [width, width + state], axis=1)
    x_act = causal_silu(jnp.concatenate([tail_x, x_in], axis=0), conv_x, length)
    b_act = causal_silu(jnp.concatenate([tail_b, b_in], axis=0), conv_b, length)
    c_act = causal_silu(jnp.concatenate([tail_c, c_in], axis=0), conv_c, length)
    delta = jax.nn.softplus(dt_raw + dt_bias)
    rates = -jnp.exp(a_log) * delta
    lower = jnp.tril(jnp.ones((SPAN, SPAN), dtype=bool))
    logs = jnp.dot(
        lower.astype(jnp.float32), rates, precision=lax.Precision.HIGHEST,
        preferred_element_type=jnp.float32,
    )
    last = logs[-1]
    x_heads = x_act.reshape(length, heads, head_size)
    x_wide = x_heads.astype(jnp.float32)
    scaled = ((jnp.exp(last - logs) * delta)[..., None] * x_wide).astype(jnp.bfloat16)
    update = jnp.einsum("shp,sn->hpn", scaled, b_act, preferred_element_type=jnp.float32)
    state_low = entering_states(update, last)
    scores = jnp.dot(c_act, b_act.T, preferred_element_type=jnp.float32)
    log_rows = logs.T
    decay = jnp.exp(jnp.where(lower[None], log_rows[:, :, None] - log_rows[:, None, :], -jnp.inf))
    weights = (scores[None] * decay * delta.T[:, None, :]).astype(jnp.bfloat16)
    inner = jnp.einsum("hts,shp->thp", weights, x_heads, preferred_element_type=jnp.float32)
    outer = jnp.einsum("tn,hpn->thp", c_act, state_low, preferred_element_type=jnp.float32)
    y_val = inner + jnp.exp(logs)[..., None] * outer + d_skip[:, None] * x_wide
    gated = y_val.reshape(length, width) * jax.nn.silu(z_in.astype(jnp.float32))
    meansq = jnp.mean(gated * gated, axis=-1, keepdims=True)
    normed = (gated * lax.rsqrt(meansq + 1e-05) * norm_gain).astype(jnp.bfloat16)
    return lax.all_to_all(normed.T, "ctx", split_axis=0, concat_axis=1, tiled=True)


def solution(mesh):
    return jax.shard_map(
        shards,
        mesh=mesh,
        in_specs=(
            P("ctx", "tp"),
            P("ctx", "tp"),
            P("ctx", "tp"),
            P("ctx", "tp"),
            P("ctx", "tp"),
            P("tp"),
            P("tp"),
            P("tp"),
            P(None, "tp"),
            P(None, "tp"),
            P(None, "tp"),
            P("tp"),
        ),
        out_specs=P(("tp", "ctx"), None),
        check_vma=False,
    )
```

```python
import jax
import jax.numpy as jnp
from jax import lax
from jax.experimental import pallas as pl
from jax.experimental.pallas import tpu as pltpu
from jax.sharding import PartitionSpec as P

SPAN = 128
NEAR = 8
EXTRA = 16
LOW = 20 << 20


def split3(value):
    first = value.astype(jnp.bfloat16)
    rest = value - first.astype(jnp.float32)
    second = rest.astype(jnp.bfloat16)
    third = (rest - second.astype(jnp.float32)).astype(jnp.bfloat16)
    return [first, second, third]


def pack_tails(x_ref, b_ref, c_ref, out_ref):
    width, state = x_ref.shape[1], b_ref.shape[1]
    out_ref[:, :width] = x_ref[...]
    out_ref[:, width : width + state] = b_ref[...]
    out_ref[:, width + state :] = c_ref[...]


def conv_silu(tail, rows, taps, scratch):
    length, width = rows.shape
    back = taps.shape[0] - 1
    scratch[0:8, :width] = tail[8:16].astype(jnp.float32)
    scratch[8 : 8 + length, :width] = rows.astype(jnp.float32)
    total = taps[0:1] * scratch[8 - back : 8 - back + length, :width]
    for k in range(1, back + 1):
        total = total + taps[k : k + 1] * scratch[8 - back + k : 8 - back + k + length, :width]
    return (total / (1.0 + jnp.exp(-total))).astype(jnp.bfloat16)


def local_part(
    tail_ref, x_ref, b_ref, c_ref, dt_ref, bias_ref, alog_ref, tx_ref, tb_ref, tc_ref,
    message_ref, x_out, b_out, c_out, logs_out, delta_out, scratch,
):
    length, width = x_ref.shape
    state = b_ref.shape[1]
    heads = dt_ref.shape[0]
    b_act = conv_silu(tail_ref[:, width : width + state], b_ref[...], tb_ref[...], scratch)
    b_out[...] = b_act
    c_out[...] = conv_silu(tail_ref[:, width + state :], c_ref[...], tc_ref[...], scratch)
    raw = dt_ref[...] + bias_ref[...].T
    grown = jnp.exp(-jnp.abs(raw))
    one_more = 1.0 + grown
    ratio = grown / jnp.where(one_more == 1.0, 1.0, one_more - 1.0)
    delta = jnp.maximum(raw, 0.0) + jnp.where(one_more == 1.0, grown, jnp.log(one_more) * ratio)
    rates = -jnp.exp(alog_ref[...].T) * delta
    until = (
        lax.broadcasted_iota(jnp.int32, (length, length), 0)
        <= lax.broadcasted_iota(jnp.int32, (length, length), 1)
    ).astype(jnp.bfloat16)
    logs = jnp.zeros(rates.shape, jnp.float32)
    for part in split3(rates):
        logs = logs + jnp.dot(part, until, preferred_element_type=jnp.float32)
    last = logs[:, length - 1 : length]
    logs_out[...] = logs
    delta_out[...] = delta
    scale = (jnp.exp(last - logs) * delta).T
    decay = [part.astype(jnp.float32) for part in split3(jnp.exp(last))]
    lane = lax.broadcasted_iota(jnp.int32, (length, 128), 1)
    row = lax.broadcasted_iota(jnp.int32, (EXTRA, 128), 0)
    for p in range(width // 128):
        here = slice(128 * p, 128 * p + 128)
        x_act = conv_silu(tail_ref[:, here], x_ref[:, here], tx_ref[:, here], scratch)
        x_out[:, here] = x_act
        factor = jnp.where(lane < 64, scale[:, 2 * p : 2 * p + 1], scale[:, 2 * p + 1 : 2 * p + 2])
        scaled = (factor * x_act.astype(jnp.float32)).astype(jnp.bfloat16)
        update = lax.dot_general(
            scaled, b_act, (((0,), (0,)), ((), ())), preferred_element_type=jnp.float32
        )
        message_ref[p, 0:128, :] = update.astype(jnp.bfloat16)
        extra = jnp.zeros((EXTRA, 128), jnp.float32)
        for k in range(6):
            h = 2 * p + k % 2
            extra = jnp.where(row == k, decay[k // 2][h : h + 1, :], extra)
        message_ref[p, 128 : 128 + EXTRA, :] = extra.astype(jnp.bfloat16)


def read_decays(message):
    parts = message[..., 128:134, :].astype(jnp.float32)
    return parts[..., 0:2, :] + parts[..., 2:4, :] + parts[..., 4:6, :]


def widen(decay):
    return jnp.repeat(decay, 64, axis=-2)


def entering_states(message):
    count = lax.axis_size("ctx")
    groups = count // NEAR
    near = [list(range(g * NEAR, (g + 1) * NEAR)) for g in range(groups)]
    message = lax.all_to_all(message, "ctx", 0, 0, tiled=True, axis_index_groups=near)
    parts = message[:, :128].astype(jnp.float32)
    part_decays = read_decays(message)
    inside, decays = [jnp.zeros((128, 128), jnp.float32)], [jnp.ones((2, 128), jnp.float32)]
    for k in range(NEAR):
        inside.append(widen(part_decays[k]) * inside[-1] + parts[k])
        decays.append(decays[-1] * part_decays[k])
    total, decay = inside[NEAR], widen(decays[NEAR])
    before = jnp.zeros((128, 128), jnp.float32)
    came = jnp.zeros((128, 128), jnp.bfloat16)
    for g in range(groups - 1):
        on = (decay * came.astype(jnp.float32) + total).astype(jnp.bfloat16)
        came = lax.ppermute(on, "ctx", [(i, i + NEAR) for i in near[g]])
        before = before + came.astype(jnp.float32)
    inside = lax.optimization_barrier(jnp.stack(inside[:NEAR]))
    decays = lax.optimization_barrier(jnp.stack(decays[:NEAR]))
    states = (inside + widen(decays) * before).astype(jnp.bfloat16)
    states = lax.all_to_all(states, "ctx", 0, 0, tiled=True, axis_index_groups=near)
    return states.reshape(NEAR * 128, 128)


def shards(
    x_in, z_in, b_in, c_in, dt_raw, dt_bias, a_log, d_skip, conv_x, conv_b, conv_c, norm_gain
):
    length, width = x_in.shape
    heads = dt_raw.shape[1]
    head_size = width // heads
    state = b_in.shape[1]
    count = lax.axis_size("ctx")
    whole = width + 2 * state
    f32, bf16 = jnp.float32, jnp.bfloat16
    end = length // 16 - 1
    tails = pl.pallas_call(
        pack_tails,
        grid=(1,),
        in_specs=[pl.BlockSpec((16, v), lambda i: (end, 0)) for v in (width, state, state)],
        out_specs=pl.BlockSpec((16, whole), lambda i: (0, 0)),
        out_shape=jax.ShapeDtypeStruct((16, whole), bf16),
        name="pack_tails",
    )(x_in, b_in, c_in)
    tails = lax.ppermute(tails, "ctx", [(i, i + 1) for i in range(count - 1)])
    message, x_act, b_act, c_act, logs, delta = pl.pallas_call(
        local_part,
        out_shape=[
            jax.ShapeDtypeStruct((width // 128, 128 + EXTRA, state), bf16),
            jax.ShapeDtypeStruct((length, width), bf16),
            jax.ShapeDtypeStruct((length, state), bf16),
            jax.ShapeDtypeStruct((length, state), bf16),
            jax.ShapeDtypeStruct((heads, length), f32),
            jax.ShapeDtypeStruct((heads, length), f32),
        ],
        scratch_shapes=[pltpu.VMEM((8 + length, 128), f32)],
        compiler_params=pltpu.CompilerParams(vmem_limit_bytes=LOW),
        name="local_part",
    )(
        tails, x_in, b_in, c_in, dt_raw.T, dt_bias[None], a_log[None], conv_x, conv_b, conv_c
    )
    lower = jnp.triu(jnp.ones((SPAN, SPAN), dtype=bool))
    x_heads = x_act.T.reshape(heads, head_size, length)
    scores = jnp.dot(b_act, c_act.T, preferred_element_type=f32)
    decay = jnp.exp(jnp.where(lower[None], logs[:, None, :] - logs[:, :, None], -jnp.inf))
    weights = (scores[None] * decay * delta[:, :, None]).astype(bf16)
    inner = jnp.einsum("hst,hps->hpt", weights, x_heads, preferred_element_type=f32)
    inner = inner + d_skip[:, None, None] * x_heads.astype(f32)
    gate = jax.nn.silu(z_in.astype(f32)).T
    gain = gate * norm_gain[:, None]
    inner, gate, gain, grown = lax.optimization_barrier((inner, gate, gain, jnp.exp(logs)))
    state_low = entering_states(message)
    outer = jnp.dot(state_low, c_act.T, preferred_element_type=f32)
    y_val = inner + grown[:, None, :] * outer.reshape(heads, head_size, length)
    y_val = y_val.reshape(width, length)
    gated = y_val * gate
    meansq = jnp.mean(gated * gated, axis=0, keepdims=True)
    normed = (y_val * gain * lax.rsqrt(meansq + 1e-05)).astype(bf16)
    return lax.all_to_all(normed, "ctx", split_axis=0, concat_axis=1, tiled=True)


def solution(mesh):
    return jax.shard_map(
        shards,
        mesh=mesh,
        in_specs=(
            P("ctx", "tp"),
            P("ctx", "tp"),
            P("ctx", "tp"),
            P("ctx", "tp"),
            P("ctx", "tp"),
            P("tp"),
            P("tp"),
            P("tp"),
            P(None, "tp"),
            P(None, "tp"),
            P(None, "tp"),
            P("tp"),
        ),
        out_specs=P(("tp", "ctx"), None),
        check_vma=False,
    )
```

```python
import jax
import jax.numpy as jnp
from jax import lax
from jax.experimental import pallas as pl
from jax.experimental.pallas import tpu as pltpu
from jax.sharding import PartitionSpec as P

SPAN = 128
NEAR = 8
EXTRA = 32
LOW = 20 << 20
HIGH = 56 << 20


def split3(value):
    first = value.astype(jnp.bfloat16)
    rest = value - first.astype(jnp.float32)
    second = rest.astype(jnp.bfloat16)
    third = (rest - second.astype(jnp.float32)).astype(jnp.bfloat16)
    return [first, second, third]


def pack_tails(x_ref, b_ref, c_ref, out_ref):
    width, state = x_ref.shape[1], b_ref.shape[1]
    out_ref[:, :width] = x_ref[...]
    out_ref[:, width : width + state] = b_ref[...]
    out_ref[:, width + state :] = c_ref[...]


def conv_silu(tail, rows, taps, scratch):
    length, width = rows.shape
    back = taps.shape[0] - 1
    scratch[0:8, :width] = tail.astype(jnp.float32)
    scratch[8 : 8 + length, :width] = rows.astype(jnp.float32)
    total = taps[0:1] * scratch[8 - back : 8 - back + length, :width]
    for k in range(1, back + 1):
        total = total + taps[k : k + 1] * scratch[8 - back + k : 8 - back + k + length, :width]
    return (total / (1.0 + jnp.exp(-total))).astype(jnp.bfloat16)


def without_halo(
    x_ref, b_ref, dt_ref, bias_ref, alog_ref, tx_ref, tb_ref,
    message_ref, logs_out, delta_out, scratch, b_scratch, extra,
):
    length, width = x_ref.shape
    back = tx_ref.shape[0] - 1
    nothing = jnp.zeros((8, 128), jnp.bfloat16)
    b_act = conv_silu(nothing, b_ref[...], tb_ref[...], b_scratch)
    raw = dt_ref[...] + bias_ref[...].T
    grown = jnp.exp(-jnp.abs(raw))
    one_more = 1.0 + grown
    ratio = grown / jnp.where(one_more == 1.0, 1.0, one_more - 1.0)
    delta = jnp.maximum(raw, 0.0) + jnp.where(one_more == 1.0, grown, jnp.log(one_more) * ratio)
    rates = -jnp.exp(alog_ref[...].T) * delta
    until = (
        lax.broadcasted_iota(jnp.int32, (length, length), 0)
        <= lax.broadcasted_iota(jnp.int32, (length, length), 1)
    ).astype(jnp.bfloat16)
    logs = jnp.zeros(rates.shape, jnp.float32)
    for part in split3(rates):
        logs = logs + jnp.dot(part, until, preferred_element_type=jnp.float32)
    last = logs[:, length - 1 : length]
    logs_out[...] = logs
    delta_out[...] = delta
    scale = (jnp.exp(last - logs) * delta).T
    decay = [part.astype(jnp.float32) for part in split3(jnp.exp(last))]
    lane = lax.broadcasted_iota(jnp.int32, (length, 128), 1)
    late = lax.broadcasted_iota(jnp.int32, (length, 128), 0) >= back
    extra[...] = jnp.zeros(extra.shape, jnp.float32)
    for p in range(width // 128):
        here = slice(128 * p, 128 * p + 128)
        x_act = conv_silu(nothing, x_ref[:, here], tx_ref[:, here], scratch)
        factor = jnp.where(lane < 64, scale[:, 2 * p : 2 * p + 1], scale[:, 2 * p + 1 : 2 * p + 2])
        scaled = jnp.where(late, factor * x_act.astype(jnp.float32), 0.0).astype(jnp.bfloat16)
        update = lax.dot_general(
            scaled, b_act, (((0,), (0,)), ((), ())), preferred_element_type=jnp.float32
        )
        message_ref[p, 0:128, :] = update.astype(jnp.bfloat16)
        for k in range(6):
            h = 2 * p + k % 2
            extra[k : k + 1, :] = jnp.broadcast_to(decay[k // 2][h : h + 1, :], (1, 128))
        extra[6:9, :] = scratch[8:11, :]
        extra[9:12, :] = scratch[5 + length : 8 + length, :]
        extra[12:15, :] = b_scratch[8:11, :]
        extra[15:18, :] = b_scratch[5 + length : 8 + length, :]
        for k, part in enumerate(split3(factor[0:8])):
            extra[18 + 3 * k : 21 + 3 * k, :] = part.astype(jnp.float32)[0:3]
        message_ref[p, 128 : 128 + EXTRA, :] = extra[...].astype(jnp.bfloat16)


def all_rows(
    tail_ref, x_ref, b_ref, c_ref, tx_ref, tb_ref, tc_ref, x_out, b_out, c_out, scratch
):
    width, state = x_ref.shape[1], b_ref.shape[1]
    for p in range(width // 128):
        here = slice(128 * p, 128 * p + 128)
        x_out[:, here] = conv_silu(tail_ref[8:16, here], x_ref[:, here], tx_ref[:, here], scratch)
    b_out[...] = conv_silu(
        tail_ref[8:16, width : width + state], b_ref[...], tb_ref[...], scratch
    )
    c_out[...] = conv_silu(tail_ref[8:16, width + state :], c_ref[...], tc_ref[...], scratch)


def widen(decay):
    return jnp.repeat(decay, 64, axis=-2)


def own_taps(first, taps):
    return sum(
        jnp.pad(taps[k] * first[..., : k, :], [(0, 0)] * (first.ndim - 2) + [(3 - k, 0), (0, 0)])
        for k in range(1, 4)
    )


def tail_taps(tail, taps):
    return sum(
        jnp.pad(taps[k] * tail[..., k:, :], [(0, 0)] * (tail.ndim - 2) + [(0, k), (0, 0)])
        for k in range(3)
    )


def near_groups():
    count = lax.axis_size("ctx")
    return [list(range(g * NEAR, (g + 1) * NEAR)) for g in range(count // NEAR)]


def first_update(total_x, total_b, scale):
    scaled = scale * jax.nn.silu(total_x).astype(jnp.bfloat16).astype(jnp.float32)
    return jnp.einsum(
        "...tc,...tn->...cn",
        scaled.astype(jnp.bfloat16),
        jax.nn.silu(total_b).astype(jnp.bfloat16),
        preferred_element_type=jnp.float32,
    )


def entering_states(message, conv_x, conv_b):
    f32, bf16 = jnp.float32, jnp.bfloat16
    near = near_groups()
    place = lax.axis_index("ctx") % NEAR
    taps_x = lax.dynamic_slice_in_dim(conv_x, place * 128, 128, 1)
    taps_b = conv_b
    rest = message[:, 128:].astype(f32)
    part_decays = rest[:, 0:2] + rest[:, 2:4] + rest[:, 4:6]
    first_x, tail_x, first_b, tail_b = (rest[:, 6 + 3 * i : 9 + 3 * i] for i in range(4))
    scale = rest[:, 18:21] + rest[:, 21:24] + rest[:, 24:27]
    shifted = [jnp.pad(v[:-1], ((1, 0), (0, 0), (0, 0))) for v in (tail_x, tail_b)]
    parts = message[:, :128].astype(f32) + first_update(
        own_taps(first_x, taps_x) + tail_taps(shifted[0], taps_x),
        own_taps(first_b, taps_b) + tail_taps(shifted[1], taps_b),
        scale,
    )
    inside, decays = [jnp.zeros((128, 128), f32)], [jnp.ones((2, 128), f32)]
    after = [jnp.zeros((2, 128), f32), jnp.ones((2, 128), f32)]
    for k in range(NEAR):
        inside.append(widen(part_decays[k]) * inside[-1] + parts[k])
        decays.append(decays[-1] * part_decays[k])
        if k:
            after.append(after[-1] * part_decays[k])
    total, decay = inside[NEAR], widen(decays[NEAR])
    ends = message[NEAR - 1, 128 + 9 : 128 + 18]
    ends = jnp.pad(jnp.concatenate([ends[0:3], ends[6:9]], axis=0), ((0, 10), (0, 0)))
    own_x, own_b = own_taps(first_x[0], taps_x), own_taps(first_b[0], taps_b)
    without = first_update(own_x, own_b, scale[0])

    def change(rows):
        x_part, b_part = tail_taps(rows[0:3], taps_x), tail_taps(rows[3:6], taps_b)
        return first_update(own_x + x_part, own_b + b_part, scale[0])

    behind = widen(after[NEAR])
    total, base = total.astype(bf16), total - behind * without
    base, own_x, own_b, ends = lax.optimization_barrier((base, own_x, own_b, ends))
    before, rows = jnp.zeros((128, 128), f32), jnp.zeros((16, 128), f32)
    on = total
    for g in range(len(near) - 1):
        sent = jnp.concatenate([on, ends], axis=0)
        came = lax.ppermute(sent, "ctx", [(i, i + NEAR) for i in near[g]]).astype(f32)
        on = (decay * came[:128] + base + behind * change(came[128:])).astype(bf16)
        before, rows = before + came[:128], rows + came[128:]
    change = change(rows) - without
    inside = jnp.stack(inside[:NEAR]) + widen(jnp.stack(after[:NEAR])) * change
    inside = lax.optimization_barrier(inside)
    decays = lax.optimization_barrier(jnp.stack(decays[:NEAR]))
    states = (inside + widen(decays) * before).astype(bf16)
    states = lax.all_to_all(states, "ctx", 0, 0, tiled=True, axis_index_groups=near)
    return states.reshape(NEAR * 128, 128)


def halo(tails):
    count = lax.axis_size("ctx")
    return lax.ppermute(tails, "ctx", [(i, i + 1) for i in range(count - 1)])


def shards(
    x_in, z_in, b_in, c_in, dt_raw, dt_bias, a_log, d_skip, conv_x, conv_b, conv_c, norm_gain
):
    length, width = x_in.shape
    heads = dt_raw.shape[1]
    head_size = width // heads
    state = b_in.shape[1]
    count = lax.axis_size("ctx")
    whole = width + 2 * state
    f32, bf16 = jnp.float32, jnp.bfloat16
    shape = jax.ShapeDtypeStruct
    message, logs, delta = pl.pallas_call(
        without_halo,
        out_shape=[
            shape((width // 128, 128 + EXTRA, state), bf16),
            shape((heads, length), f32),
            shape((heads, length), f32),
        ],
        scratch_shapes=[
            pltpu.VMEM((8 + length, 128), f32),
            pltpu.VMEM((8 + length, 128), f32),
            pltpu.VMEM((EXTRA, 128), f32),
        ],
        compiler_params=pltpu.CompilerParams(vmem_limit_bytes=HIGH),
        name="without_halo",
    )(x_in, b_in, dt_raw.T, dt_bias[None], a_log[None], conv_x, conv_b)
    late_x, late_b, late_c, _ = lax.optimization_barrier((x_in, b_in, c_in, message))
    end = length // 16 - 1
    tails = pl.pallas_call(
        pack_tails,
        grid=(1,),
        in_specs=[pl.BlockSpec((16, v), lambda i: (end, 0)) for v in (width, state, state)],
        out_specs=pl.BlockSpec((16, whole), lambda i: (0, 0)),
        out_shape=shape((16, whole), bf16),
        name="pack_tails",
    )(late_x, late_b, late_c)
    tails = halo(tails)
    x_act, b_act, c_act = pl.pallas_call(
        all_rows,
        out_shape=[shape((length, v), bf16) for v in (width, state, state)],
        scratch_shapes=[pltpu.VMEM((8 + length, 128), f32)],
        compiler_params=pltpu.CompilerParams(vmem_limit_bytes=LOW),
        name="all_rows",
    )(tails, late_x, late_b, late_c, conv_x, conv_b, conv_c)
    message = lax.all_to_all(message, "ctx", 0, 0, tiled=True, axis_index_groups=near_groups())
    message, x_act, b_act, c_act = lax.optimization_barrier((message, x_act, b_act, c_act))
    lower = jnp.triu(jnp.ones((SPAN, SPAN), dtype=bool))
    x_heads = x_act.T.reshape(heads, head_size, length)
    scores = jnp.dot(b_act, c_act.T, preferred_element_type=f32)
    decay = jnp.exp(jnp.where(lower[None], logs[:, None, :] - logs[:, :, None], -jnp.inf))
    weights = (scores[None] * decay * delta[:, :, None]).astype(bf16)
    inner = jnp.einsum("hst,hps->hpt", weights, x_heads, preferred_element_type=f32)
    inner = inner + d_skip[:, None, None] * x_heads.astype(f32)
    gate = jax.nn.silu(z_in.astype(f32)).T
    gain = gate * norm_gain[:, None]
    inner, gate, gain, grown = lax.optimization_barrier((inner, gate, gain, jnp.exp(logs)))
    state_low = entering_states(message, conv_x, conv_b)
    outer = jnp.dot(state_low, c_act.T, preferred_element_type=f32)
    y_val = inner + grown[:, None, :] * outer.reshape(heads, head_size, length)
    y_val = y_val.reshape(width, length)
    gated = y_val * gate
    meansq = jnp.mean(gated * gated, axis=0, keepdims=True)
    normed = (y_val * gain * lax.rsqrt(meansq + 1e-05)).astype(bf16)
    return lax.all_to_all(normed, "ctx", split_axis=0, concat_axis=1, tiled=True)


def solution(mesh):
    return jax.shard_map(
        shards,
        mesh=mesh,
        in_specs=(
            P("ctx", "tp"),
            P("ctx", "tp"),
            P("ctx", "tp"),
            P("ctx", "tp"),
            P("ctx", "tp"),
            P("tp"),
            P("tp"),
            P("tp"),
            P(None, "tp"),
            P(None, "tp"),
            P(None, "tp"),
            P("tp"),
        ),
        out_specs=P(("tp", "ctx"), None),
        check_vma=False,
    )
```

```python
import jax
import jax.numpy as jnp
from jax import lax
from jax.experimental import pallas as pl
from jax.experimental.pallas import tpu as pltpu
from jax.sharding import PartitionSpec as P

SPAN = 128
NEAR = 8
EXTRA = 32
LOW = 20 << 20
HIGH = 56 << 20


def split3(value):
    first = value.astype(jnp.bfloat16)
    rest = value - first.astype(jnp.float32)
    second = rest.astype(jnp.bfloat16)
    third = (rest - second.astype(jnp.float32)).astype(jnp.bfloat16)
    return [first, second, third]


def pack_tails(x_ref, b_ref, c_ref, out_ref):
    width, state = x_ref.shape[1], b_ref.shape[1]
    out_ref[:, :width] = x_ref[...]
    out_ref[:, width : width + state] = b_ref[...]
    out_ref[:, width + state :] = c_ref[...]


def conv_silu(tail, rows, taps, scratch):
    length, width = rows.shape
    back = taps.shape[0] - 1
    scratch[0:8, :width] = tail.astype(jnp.float32)
    scratch[8 : 8 + length, :width] = rows.astype(jnp.float32)
    total = taps[0:1] * scratch[8 - back : 8 - back + length, :width]
    for k in range(1, back + 1):
        total = total + taps[k : k + 1] * scratch[8 - back + k : 8 - back + k + length, :width]
    return (total / (1.0 + jnp.exp(-total))).astype(jnp.bfloat16)


def without_halo(
    x_ref, b_ref, dt_ref, bias_ref, alog_ref, tx_ref, tb_ref,
    message_ref, logs_out, delta_out, scratch, b_scratch, extra,
):
    length, width = x_ref.shape
    back = tx_ref.shape[0] - 1
    nothing = jnp.zeros((8, 128), jnp.bfloat16)
    b_act = conv_silu(nothing, b_ref[...], tb_ref[...], b_scratch)
    raw = dt_ref[...] + bias_ref[...].T
    grown = jnp.exp(-jnp.abs(raw))
    one_more = 1.0 + grown
    ratio = grown / jnp.where(one_more == 1.0, 1.0, one_more - 1.0)
    delta = jnp.maximum(raw, 0.0) + jnp.where(one_more == 1.0, grown, jnp.log(one_more) * ratio)
    rates = -jnp.exp(alog_ref[...].T) * delta
    until = (
        lax.broadcasted_iota(jnp.int32, (length, length), 0)
        <= lax.broadcasted_iota(jnp.int32, (length, length), 1)
    ).astype(jnp.bfloat16)
    logs = jnp.zeros(rates.shape, jnp.float32)
    for part in split3(rates):
        logs = logs + jnp.dot(part, until, preferred_element_type=jnp.float32)
    last = logs[:, length - 1 : length]
    logs_out[...] = logs
    delta_out[...] = delta
    scale = (jnp.exp(last - logs) * delta).T
    decay = [part.astype(jnp.float32) for part in split3(jnp.exp(last))]
    lane = lax.broadcasted_iota(jnp.int32, (length, 128), 1)
    late = lax.broadcasted_iota(jnp.int32, (length, 128), 0) >= back
    extra[...] = jnp.zeros(extra.shape, jnp.float32)
    for p in range(width // 128):
        here = slice(128 * p, 128 * p + 128)
        x_act = conv_silu(nothing, x_ref[:, here], tx_ref[:, here], scratch)
        factor = jnp.where(lane < 64, scale[:, 2 * p : 2 * p + 1], scale[:, 2 * p + 1 : 2 * p + 2])
        scaled = jnp.where(late, factor * x_act.astype(jnp.float32), 0.0).astype(jnp.bfloat16)
        update = lax.dot_general(
            scaled, b_act, (((0,), (0,)), ((), ())), preferred_element_type=jnp.float32
        )
        message_ref[p, 0:128, :] = update.astype(jnp.bfloat16)
        for k in range(6):
            h = 2 * p + k % 2
            extra[k : k + 1, :] = jnp.broadcast_to(decay[k // 2][h : h + 1, :], (1, 128))
        extra[6:9, :] = scratch[8:11, :]
        extra[9:12, :] = scratch[5 + length : 8 + length, :]
        extra[12:15, :] = b_scratch[8:11, :]
        extra[15:18, :] = b_scratch[5 + length : 8 + length, :]
        for k, part in enumerate(split3(factor[0:8])):
            extra[18 + 3 * k : 21 + 3 * k, :] = part.astype(jnp.float32)[0:3]
        message_ref[p, 128 : 128 + EXTRA, :] = extra[...].astype(jnp.bfloat16)


def all_rows(
    tail_ref, x_ref, b_ref, c_ref, tx_ref, tb_ref, tc_ref, x_out, b_out, c_out, scratch
):
    width, state = x_ref.shape[1], b_ref.shape[1]
    for p in range(width // 128):
        here = slice(128 * p, 128 * p + 128)
        x_out[:, here] = conv_silu(tail_ref[8:16, here], x_ref[:, here], tx_ref[:, here], scratch)
    b_out[...] = conv_silu(
        tail_ref[8:16, width : width + state], b_ref[...], tb_ref[...], scratch
    )
    c_out[...] = conv_silu(tail_ref[8:16, width + state :], c_ref[...], tc_ref[...], scratch)


def widen(decay):
    return jnp.repeat(decay, 64, axis=-2)


def own_taps(first, taps):
    return sum(
        jnp.pad(taps[k] * first[..., : k, :], [(0, 0)] * (first.ndim - 2) + [(3 - k, 0), (0, 0)])
        for k in range(1, 4)
    )


def tail_taps(tail, taps):
    return sum(
        jnp.pad(taps[k] * tail[..., k:, :], [(0, 0)] * (tail.ndim - 2) + [(0, k), (0, 0)])
        for k in range(3)
    )


def near_groups():
    count = lax.axis_size("ctx")
    return [list(range(g * NEAR, (g + 1) * NEAR)) for g in range(count // NEAR)]


def first_update(total_x, total_b, scale):
    scaled = scale * jax.nn.silu(total_x).astype(jnp.bfloat16).astype(jnp.float32)
    return jnp.einsum(
        "...tc,...tn->...cn",
        scaled.astype(jnp.bfloat16),
        jax.nn.silu(total_b).astype(jnp.bfloat16),
        preferred_element_type=jnp.float32,
    )


def entering_states(message, conv_x, conv_b):
    f32, bf16 = jnp.float32, jnp.bfloat16
    near = near_groups()
    place = lax.axis_index("ctx") % NEAR
    taps_x = lax.dynamic_slice_in_dim(conv_x, place * 128, 128, 1)
    taps_b = conv_b
    rest = message[:, 128:].astype(f32)
    part_decays = rest[:, 0:2] + rest[:, 2:4] + rest[:, 4:6]
    first_x, tail_x, first_b, tail_b = (rest[:, 6 + 3 * i : 9 + 3 * i] for i in range(4))
    scale = rest[:, 18:21] + rest[:, 21:24] + rest[:, 24:27]
    shifted = [jnp.pad(v[:-1], ((1, 0), (0, 0), (0, 0))) for v in (tail_x, tail_b)]
    parts = message[:, :128].astype(f32) + first_update(
        own_taps(first_x, taps_x) + tail_taps(shifted[0], taps_x),
        own_taps(first_b, taps_b) + tail_taps(shifted[1], taps_b),
        scale,
    )
    inside, decays = [jnp.zeros((128, 128), f32)], [jnp.ones((2, 128), f32)]
    after = [jnp.zeros((2, 128), f32), jnp.ones((2, 128), f32)]
    for k in range(NEAR):
        inside.append(widen(part_decays[k]) * inside[-1] + parts[k])
        decays.append(decays[-1] * part_decays[k])
        if k:
            after.append(after[-1] * part_decays[k])
    total, decay = inside[NEAR], widen(decays[NEAR])
    block = message[NEAR - 1, 128 + 9 : 128 + 18]
    ends = jnp.pad(jnp.concatenate([block[0:3], block[6:9]], axis=0), ((0, 10), (0, 0)))
    known = (own_taps(first_x[0], taps_x), own_taps(first_b[0], taps_b), scale[0])
    without = first_update(*known)

    def change(rows, own_x, own_b, scale):
        x_part, b_part = tail_taps(rows[0:3], taps_x), tail_taps(rows[3:6], taps_b)
        return first_update(own_x + x_part, own_b + b_part, scale)

    def send(value, pairs):
        pairs = [(i, i + NEAR * (t - g)) for g, t in pairs for i in near[g]]
        return lax.ppermute(value, "ctx", pairs)

    behind = widen(after[NEAR])
    base = total - behind * without
    came = send(jnp.concatenate([total.astype(bf16), ends], axis=0), [(0, 1)]).astype(f32)
    entry, rows = came[:128], came[128:]
    base, known, ends = lax.optimization_barrier((base, known, ends))
    half = len(near) // 2
    for g in range(1, half):
        on = (decay * came[:128] + base + behind * change(came[128:], *known)).astype(bf16)
        sent = jnp.concatenate([on, ends], axis=0)
        if g < half - 1:
            came = send(sent, [(g, g + 1)])
            if g == 1:
                base_low, came = lax.optimization_barrier((base.astype(bf16), came))
            came = came.astype(f32)
            entry, rows = entry + came[:128], rows + came[128:]
    thirds = [
        lax.reduce_precision(v, 8, 7)
        for d in (decays[NEAR], after[NEAR])
        for v in (d, d - lax.reduce_precision(d, 8, 7))
    ]
    extra = [first_x[0], first_b[0], *(rest[0, 18 + 3 * i : 21 + 3 * i] for i in range(3)), *thirds]
    extra = jnp.concatenate(extra, axis=0).astype(bf16)
    extra = jnp.pad(extra, ((0, 32 - extra.shape[0]), (0, 0)))
    even = jnp.concatenate([base_low, ends, extra], axis=0)
    groups = len(near)
    even = send(even, [(g, g + 1) for g in range(half, groups, 2)])
    far = jnp.zeros((144, 128), f32)
    for g in range(half - 1, groups - 1, 2):
        sent = jnp.concatenate([on, ends], axis=0)
        came = send(sent, [(g, g + 2)])
        if g == groups - 3:
            sent, came = lax.optimization_barrier((sent, came))
        if g == half - 1:
            even, came = lax.optimization_barrier((even, came))
            even = even.astype(f32)
            base_e, ends_e, extra = even[:128], even[128:144], even[144:]
            known_e = (
                own_taps(extra[0:3], taps_x),
                own_taps(extra[3:6], taps_b),
                extra[6:9] + extra[9:12] + extra[12:15],
            )
            decay_e = widen(extra[15:17] + extra[17:19])
            behind_e = widen(extra[19:21] + extra[21:23])
            rows = rows + ends_e
            odd = (decay * decay_e, decay * base_e + base + behind * change(ends_e, *known))
            odd = lax.optimization_barrier((*odd, decay * behind_e, decay_e, base_e, behind_e, known_e))
            step, own, first_e, decay_e, base_e, behind_e, known_e = odd
        came = came.astype(f32)
        beside = send(sent, [(g, g + 1)]).astype(f32)
        entry, rows, far = entry + beside[:128], rows + beside[128:], far + came
        on = (step * came[:128] + own + first_e * change(came[128:], *known_e)).astype(bf16)
    inside = jnp.stack(inside[:NEAR]) + widen(jnp.stack(after[:NEAR])) * (
        change(rows, *known) - without
    )
    decays = widen(jnp.stack(decays[:NEAR]))
    inside, decays, entry = lax.optimization_barrier((inside, decays, entry + base_e))
    before = entry + decay_e * far[:128] + behind_e * change(far[128:], *known_e)
    states = (inside + decays * before).astype(bf16)
    states = lax.all_to_all(states, "ctx", 0, 0, tiled=True, axis_index_groups=near)
    return states.reshape(NEAR * 128, 128)


def halo(tails):
    count = lax.axis_size("ctx")
    return lax.ppermute(tails, "ctx", [(i, i + 1) for i in range(count - 1)])


def shards(
    x_in, z_in, b_in, c_in, dt_raw, dt_bias, a_log, d_skip, conv_x, conv_b, conv_c, norm_gain
):
    length, width = x_in.shape
    heads = dt_raw.shape[1]
    head_size = width // heads
    state = b_in.shape[1]
    count = lax.axis_size("ctx")
    whole = width + 2 * state
    f32, bf16 = jnp.float32, jnp.bfloat16
    shape = jax.ShapeDtypeStruct
    message, logs, delta = pl.pallas_call(
        without_halo,
        out_shape=[
            shape((width // 128, 128 + EXTRA, state), bf16),
            shape((heads, length), f32),
            shape((heads, length), f32),
        ],
        scratch_shapes=[
            pltpu.VMEM((8 + length, 128), f32),
            pltpu.VMEM((8 + length, 128), f32),
            pltpu.VMEM((EXTRA, 128), f32),
        ],
        compiler_params=pltpu.CompilerParams(vmem_limit_bytes=HIGH),
        name="without_halo",
    )(x_in, b_in, dt_raw.T, dt_bias[None], a_log[None], conv_x, conv_b)
    late_x, late_b, late_c, _ = lax.optimization_barrier((x_in, b_in, c_in, message))
    end = length // 16 - 1
    tails = pl.pallas_call(
        pack_tails,
        grid=(1,),
        in_specs=[pl.BlockSpec((16, v), lambda i: (end, 0)) for v in (width, state, state)],
        out_specs=pl.BlockSpec((16, whole), lambda i: (0, 0)),
        out_shape=shape((16, whole), bf16),
        name="pack_tails",
    )(late_x, late_b, late_c)
    tails = halo(tails)
    x_act, b_act, c_act = pl.pallas_call(
        all_rows,
        out_shape=[shape((length, v), bf16) for v in (width, state, state)],
        scratch_shapes=[pltpu.VMEM((8 + length, 128), f32)],
        compiler_params=pltpu.CompilerParams(vmem_limit_bytes=LOW),
        name="all_rows",
    )(tails, late_x, late_b, late_c, conv_x, conv_b, conv_c)
    message = lax.all_to_all(message, "ctx", 0, 0, tiled=True, axis_index_groups=near_groups())
    message, x_act, b_act, c_act = lax.optimization_barrier((message, x_act, b_act, c_act))
    lower = jnp.triu(jnp.ones((SPAN, SPAN), dtype=bool))
    x_heads = x_act.T.reshape(heads, head_size, length)
    scores = jnp.dot(b_act, c_act.T, preferred_element_type=f32)
    decay = jnp.exp(jnp.where(lower[None], logs[:, None, :] - logs[:, :, None], -jnp.inf))
    weights = (scores[None] * decay * delta[:, :, None]).astype(bf16)
    inner = jnp.einsum("hst,hps->hpt", weights, x_heads, preferred_element_type=f32)
    inner = inner + d_skip[:, None, None] * x_heads.astype(f32)
    gate = jax.nn.silu(z_in.astype(f32)).T
    gain = gate * norm_gain[:, None]
    inner, gate, gain, grown = lax.optimization_barrier((inner, gate, gain, jnp.exp(logs)))
    state_low = entering_states(message, conv_x, conv_b)
    outer = jnp.dot(state_low, c_act.T, preferred_element_type=f32)
    y_val = inner + grown[:, None, :] * outer.reshape(heads, head_size, length)
    y_val = y_val.reshape(width, length)
    gated = y_val * gate
    meansq = jnp.mean(gated * gated, axis=0, keepdims=True)
    normed = (y_val * gain * lax.rsqrt(meansq + 1e-05)).astype(bf16)
    return lax.all_to_all(normed, "ctx", split_axis=0, concat_axis=1, tiled=True)


def solution(mesh):
    return jax.shard_map(
        shards,
        mesh=mesh,
        in_specs=(
            P("ctx", "tp"),
            P("ctx", "tp"),
            P("ctx", "tp"),
            P("ctx", "tp"),
            P("ctx", "tp"),
            P("tp"),
            P("tp"),
            P("tp"),
            P(None, "tp"),
            P(None, "tp"),
            P(None, "tp"),
            P("tp"),
        ),
        out_specs=P(("tp", "ctx"), None),
        check_vma=False,
    )
```

```python
import jax
import jax.numpy as jnp
from jax import lax
from jax.experimental import pallas as pl
from jax.experimental.pallas import tpu as pltpu
from jax.sharding import PartitionSpec as P

SPAN = 128
NEAR = 8
EXTRA = 32
LOW = 20 << 20
HIGH = 56 << 20


def split3(value):
    first = value.astype(jnp.bfloat16)
    rest = value - first.astype(jnp.float32)
    second = rest.astype(jnp.bfloat16)
    third = (rest - second.astype(jnp.float32)).astype(jnp.bfloat16)
    return [first, second, third]


def pack_tails(x_ref, b_ref, c_ref, out_ref):
    width, state = x_ref.shape[1], b_ref.shape[1]
    out_ref[:, :width] = x_ref[...]
    out_ref[:, width : width + state] = b_ref[...]
    out_ref[:, width + state :] = c_ref[...]


def conv_silu(tail, rows, taps, scratch):
    length, width = rows.shape
    back = taps.shape[0] - 1
    scratch[0:8, :width] = tail.astype(jnp.float32)
    scratch[8 : 8 + length, :width] = rows.astype(jnp.float32)
    total = taps[0:1] * scratch[8 - back : 8 - back + length, :width]
    for k in range(1, back + 1):
        total = total + taps[k : k + 1] * scratch[8 - back + k : 8 - back + k + length, :width]
    return (total / (1.0 + jnp.exp(-total))).astype(jnp.bfloat16)


def without_halo(
    x_ref, b_ref, dt_ref, bias_ref, alog_ref, tx_ref, tb_ref,
    message_ref, logs_out, delta_out, scratch, b_scratch, extra,
):
    length, width = x_ref.shape
    back = tx_ref.shape[0] - 1
    nothing = jnp.zeros((8, 128), jnp.bfloat16)
    b_act = conv_silu(nothing, b_ref[...], tb_ref[...], b_scratch)
    raw = dt_ref[...] + bias_ref[...].T
    grown = jnp.exp(-jnp.abs(raw))
    one_more = 1.0 + grown
    ratio = grown / jnp.where(one_more == 1.0, 1.0, one_more - 1.0)
    delta = jnp.maximum(raw, 0.0) + jnp.where(one_more == 1.0, grown, jnp.log(one_more) * ratio)
    rates = -jnp.exp(alog_ref[...].T) * delta
    until = (
        lax.broadcasted_iota(jnp.int32, (length, length), 0)
        <= lax.broadcasted_iota(jnp.int32, (length, length), 1)
    ).astype(jnp.bfloat16)
    logs = jnp.zeros(rates.shape, jnp.float32)
    for part in split3(rates):
        logs = logs + jnp.dot(part, until, preferred_element_type=jnp.float32)
    last = logs[:, length - 1 : length]
    logs_out[...] = logs
    delta_out[...] = delta
    scale = (jnp.exp(last - logs) * delta).T
    decay = [part.astype(jnp.float32) for part in split3(jnp.exp(last))]
    lane = lax.broadcasted_iota(jnp.int32, (length, 128), 1)
    late = lax.broadcasted_iota(jnp.int32, (length, 128), 0) >= back
    extra[...] = jnp.zeros(extra.shape, jnp.float32)
    for p in range(width // 128):
        here = slice(128 * p, 128 * p + 128)
        x_act = conv_silu(nothing, x_ref[:, here], tx_ref[:, here], scratch)
        factor = jnp.where(lane < 64, scale[:, 2 * p : 2 * p + 1], scale[:, 2 * p + 1 : 2 * p + 2])
        scaled = jnp.where(late, factor * x_act.astype(jnp.float32), 0.0).astype(jnp.bfloat16)
        update = lax.dot_general(
            scaled, b_act, (((0,), (0,)), ((), ())), preferred_element_type=jnp.float32
        )
        message_ref[p, 0:128, :] = update.astype(jnp.bfloat16)
        for k in range(6):
            h = 2 * p + k % 2
            extra[k : k + 1, :] = jnp.broadcast_to(decay[k // 2][h : h + 1, :], (1, 128))
        extra[6:9, :] = scratch[8:11, :]
        extra[9:12, :] = scratch[5 + length : 8 + length, :]
        extra[12:15, :] = b_scratch[8:11, :]
        extra[15:18, :] = b_scratch[5 + length : 8 + length, :]
        for k, part in enumerate(split3(factor[0:8])):
            extra[18 + 3 * k : 21 + 3 * k, :] = part.astype(jnp.float32)[0:3]
        message_ref[p, 128 : 128 + EXTRA, :] = extra[...].astype(jnp.bfloat16)


def all_rows(
    tail_ref, x_ref, b_ref, c_ref, tx_ref, tb_ref, tc_ref, x_out, b_out, c_out, scratch
):
    width, state = x_ref.shape[1], b_ref.shape[1]
    for p in range(width // 128):
        here = slice(128 * p, 128 * p + 128)
        x_out[:, here] = conv_silu(tail_ref[8:16, here], x_ref[:, here], tx_ref[:, here], scratch)
    b_out[...] = conv_silu(
        tail_ref[8:16, width : width + state], b_ref[...], tb_ref[...], scratch
    )
    c_out[...] = conv_silu(tail_ref[8:16, width + state :], c_ref[...], tc_ref[...], scratch)


def widen(decay):
    return jnp.repeat(decay, 64, axis=-2)


def own_taps(first, taps):
    return sum(
        jnp.pad(taps[k] * first[..., : k, :], [(0, 0)] * (first.ndim - 2) + [(3 - k, 0), (0, 0)])
        for k in range(1, 4)
    )


def tail_taps(tail, taps):
    return sum(
        jnp.pad(taps[k] * tail[..., k:, :], [(0, 0)] * (tail.ndim - 2) + [(0, k), (0, 0)])
        for k in range(3)
    )


def near_groups():
    count = lax.axis_size("ctx")
    return [list(range(g * NEAR, (g + 1) * NEAR)) for g in range(count // NEAR)]


def first_update(total_x, total_b, scale):
    scaled = scale * jax.nn.silu(total_x).astype(jnp.bfloat16).astype(jnp.float32)
    return jnp.einsum(
        "...tc,...tn->...cn",
        scaled.astype(jnp.bfloat16),
        jax.nn.silu(total_b).astype(jnp.bfloat16),
        preferred_element_type=jnp.float32,
    )


def entering_states(message, conv_x, conv_b, late, make_local):
    f32, bf16 = jnp.float32, jnp.bfloat16
    near = near_groups()
    place = lax.axis_index("ctx") % NEAR
    taps_x = lax.dynamic_slice_in_dim(conv_x, place * 128, 128, 1)
    taps_b = conv_b
    rest = message[:, 128:].astype(f32)
    part_decays = rest[:, 0:2] + rest[:, 2:4] + rest[:, 4:6]
    first_x, tail_x, first_b, tail_b = (rest[:, 6 + 3 * i : 9 + 3 * i] for i in range(4))
    scale = rest[:, 18:21] + rest[:, 21:24] + rest[:, 24:27]
    shifted = [jnp.pad(v[:-1], ((1, 0), (0, 0), (0, 0))) for v in (tail_x, tail_b)]
    parts = message[:, :128].astype(f32) + first_update(
        own_taps(first_x, taps_x) + tail_taps(shifted[0], taps_x),
        own_taps(first_b, taps_b) + tail_taps(shifted[1], taps_b),
        scale,
    )
    inside, decays = [jnp.zeros((128, 128), f32)], [jnp.ones((2, 128), f32)]
    after = [jnp.zeros((2, 128), f32), jnp.ones((2, 128), f32)]
    for k in range(NEAR):
        inside.append(widen(part_decays[k]) * inside[-1] + parts[k])
        decays.append(decays[-1] * part_decays[k])
        if k:
            after.append(after[-1] * part_decays[k])
    total, decay = inside[NEAR], widen(decays[NEAR])
    block = message[NEAR - 1, 128 + 9 : 128 + 18]
    ends = jnp.pad(jnp.concatenate([block[0:3], block[6:9]], axis=0), ((0, 10), (0, 0)))
    known = (own_taps(first_x[0], taps_x), own_taps(first_b[0], taps_b), scale[0])
    without = first_update(*known)

    def change(rows, own_x, own_b, scale):
        x_part, b_part = tail_taps(rows[0:3], taps_x), tail_taps(rows[3:6], taps_b)
        return first_update(own_x + x_part, own_b + b_part, scale)

    def send(value, pairs):
        pairs = [(i, i + NEAR * (t - g)) for g, t in pairs for i in near[g]]
        return lax.ppermute(value, "ctx", pairs)

    behind = widen(after[NEAR])
    base = total - behind * without
    came = send(jnp.concatenate([total.astype(bf16), ends], axis=0), [(0, 1)]).astype(f32)
    entry, rows = came[:128], came[128:]
    base, known, ends = lax.optimization_barrier((base, known, ends))
    half = len(near) // 2
    for g in range(1, half):
        on = (decay * came[:128] + base + behind * change(came[128:], *known)).astype(bf16)
        sent = jnp.concatenate([on, ends], axis=0)
        if g < half - 1:
            came = send(sent, [(g, g + 1)])
            if g == 1:
                base_low, late, came = lax.optimization_barrier((base.astype(bf16), late, came))
                local = make_local(late)
            came = came.astype(f32)
            entry, rows = entry + came[:128], rows + came[128:]
    thirds = [
        lax.reduce_precision(v, 8, 7)
        for d in (decays[NEAR], after[NEAR])
        for v in (d, d - lax.reduce_precision(d, 8, 7))
    ]
    extra = [first_x[0], first_b[0], *(rest[0, 18 + 3 * i : 21 + 3 * i] for i in range(3)), *thirds]
    extra = jnp.concatenate(extra, axis=0).astype(bf16)
    extra = jnp.pad(extra, ((0, 32 - extra.shape[0]), (0, 0)))
    even = jnp.concatenate([base_low, ends, extra], axis=0)
    groups = len(near)
    even = send(even, [(g, g + 1) for g in range(half, groups, 2)])
    far = jnp.zeros((144, 128), f32)
    for g in range(half - 1, groups - 1, 2):
        sent = jnp.concatenate([on, ends], axis=0)
        came = send(sent, [(g, g + 2)])
        if g == groups - 3:
            sent, came = lax.optimization_barrier((sent, came))
        if g == half - 1:
            even, came, local = lax.optimization_barrier((even, came, local))
            even = even.astype(f32)
            base_e, ends_e, extra = even[:128], even[128:144], even[144:]
            known_e = (
                own_taps(extra[0:3], taps_x),
                own_taps(extra[3:6], taps_b),
                extra[6:9] + extra[9:12] + extra[12:15],
            )
            decay_e = widen(extra[15:17] + extra[17:19])
            behind_e = widen(extra[19:21] + extra[21:23])
            rows = rows + ends_e
            odd = (decay * decay_e, decay * base_e + base + behind * change(ends_e, *known))
            odd = lax.optimization_barrier((*odd, decay * behind_e, decay_e, base_e, behind_e, known_e))
            step, own, first_e, decay_e, base_e, behind_e, known_e = odd
        came = came.astype(f32)
        beside = send(sent, [(g, g + 1)]).astype(f32)
        entry, rows, far = entry + beside[:128], rows + beside[128:], far + came
        on = (step * came[:128] + own + first_e * change(came[128:], *known_e)).astype(bf16)
    inside = jnp.stack(inside[:NEAR]) + widen(jnp.stack(after[:NEAR])) * (
        change(rows, *known) - without
    )
    decays = widen(jnp.stack(decays[:NEAR]))
    inside, decays, entry = lax.optimization_barrier((inside, decays, entry + base_e))
    before = entry + decay_e * far[:128] + behind_e * change(far[128:], *known_e)
    states = (inside + decays * before).astype(bf16)
    states = lax.all_to_all(states, "ctx", 0, 0, tiled=True, axis_index_groups=near)
    return states.reshape(NEAR * 128, 128), local


def halo(tails):
    count = lax.axis_size("ctx")
    return lax.ppermute(tails, "ctx", [(i, i + 1) for i in range(count - 1)])


def shards(
    x_in, z_in, b_in, c_in, dt_raw, dt_bias, a_log, d_skip, conv_x, conv_b, conv_c, norm_gain
):
    length, width = x_in.shape
    heads = dt_raw.shape[1]
    head_size = width // heads
    state = b_in.shape[1]
    count = lax.axis_size("ctx")
    whole = width + 2 * state
    f32, bf16 = jnp.float32, jnp.bfloat16
    shape = jax.ShapeDtypeStruct
    message, logs, delta = pl.pallas_call(
        without_halo,
        out_shape=[
            shape((width // 128, 128 + EXTRA, state), bf16),
            shape((heads, length), f32),
            shape((heads, length), f32),
        ],
        scratch_shapes=[
            pltpu.VMEM((8 + length, 128), f32),
            pltpu.VMEM((8 + length, 128), f32),
            pltpu.VMEM((EXTRA, 128), f32),
        ],
        compiler_params=pltpu.CompilerParams(vmem_limit_bytes=HIGH),
        name="without_halo",
    )(x_in, b_in, dt_raw.T, dt_bias[None], a_log[None], conv_x, conv_b)
    late_x, late_b, late_c, _ = lax.optimization_barrier((x_in, b_in, c_in, message))
    end = length // 16 - 1
    tails = pl.pallas_call(
        pack_tails,
        grid=(1,),
        in_specs=[pl.BlockSpec((16, v), lambda i: (end, 0)) for v in (width, state, state)],
        out_specs=pl.BlockSpec((16, whole), lambda i: (0, 0)),
        out_shape=shape((16, whole), bf16),
        name="pack_tails",
    )(late_x, late_b, late_c)
    tails = halo(tails)
    x_act, b_act, c_act = pl.pallas_call(
        all_rows,
        out_shape=[shape((length, v), bf16) for v in (width, state, state)],
        scratch_shapes=[pltpu.VMEM((8 + length, 128), f32)],
        compiler_params=pltpu.CompilerParams(vmem_limit_bytes=LOW),
        name="all_rows",
    )(tails, late_x, late_b, late_c, conv_x, conv_b, conv_c)
    message = lax.all_to_all(message, "ctx", 0, 0, tiled=True, axis_index_groups=near_groups())
    message, x_act, b_act, c_act = lax.optimization_barrier((message, x_act, b_act, c_act))
    def make_local(delta):
        lower = jnp.triu(jnp.ones((SPAN, SPAN), dtype=bool))
        x_heads = x_act.T.reshape(heads, head_size, length)
        scores = jnp.dot(b_act, c_act.T, preferred_element_type=f32)
        decay = jnp.exp(jnp.where(lower[None], logs[:, None, :] - logs[:, :, None], -jnp.inf))
        weights = (scores[None] * decay * delta[:, :, None]).astype(bf16)
        inner = jnp.einsum("hst,hps->hpt", weights, x_heads, preferred_element_type=f32)
        inner = inner + d_skip[:, None, None] * x_heads.astype(f32)
        gate = jax.nn.silu(z_in.astype(f32)).T
        return inner, gate, gate * norm_gain[:, None], jnp.exp(logs)

    state_low, local = entering_states(message, conv_x, conv_b, delta, make_local)
    inner, gate, gain, grown = local
    outer = jnp.dot(state_low, c_act.T, preferred_element_type=f32)
    y_val = inner + grown[:, None, :] * outer.reshape(heads, head_size, length)
    y_val = y_val.reshape(width, length)
    gated = y_val * gate
    meansq = jnp.mean(gated * gated, axis=0, keepdims=True)
    normed = (y_val * gain * lax.rsqrt(meansq + 1e-05)).astype(bf16)
    return lax.all_to_all(normed, "ctx", split_axis=0, concat_axis=1, tiled=True)


def solution(mesh):
    return jax.shard_map(
        shards,
        mesh=mesh,
        in_specs=(
            P("ctx", "tp"),
            P("ctx", "tp"),
            P("ctx", "tp"),
            P("ctx", "tp"),
            P("ctx", "tp"),
            P("tp"),
            P("tp"),
            P("tp"),
            P(None, "tp"),
            P(None, "tp"),
            P(None, "tp"),
            P("tp"),
        ),
        out_specs=P(("tp", "ctx"), None),
        check_vma=False,
    )
```

```python
import jax
import jax.numpy as jnp
from jax import lax
from jax.experimental import pallas as pl
from jax.experimental.pallas import tpu as pltpu
from jax.sharding import PartitionSpec as P

SPAN = 128
NEAR = 8
EXTRA = 32
LOW = 20 << 20
HIGH = 56 << 20


def split3(value):
    first = value.astype(jnp.bfloat16)
    rest = value - first.astype(jnp.float32)
    second = rest.astype(jnp.bfloat16)
    third = (rest - second.astype(jnp.float32)).astype(jnp.bfloat16)
    return [first, second, third]


def pack_tails(x_ref, b_ref, c_ref, out_ref):
    width, state = x_ref.shape[1], b_ref.shape[1]
    out_ref[:, :width] = x_ref[...]
    out_ref[:, width : width + state] = b_ref[...]
    out_ref[:, width + state :] = c_ref[...]


def conv_silu(tail, rows, taps, scratch):
    length, width = rows.shape
    back = taps.shape[0] - 1
    scratch[0:8, :width] = tail.astype(jnp.float32)
    scratch[8 : 8 + length, :width] = rows.astype(jnp.float32)
    total = taps[0:1] * scratch[8 - back : 8 - back + length, :width]
    for k in range(1, back + 1):
        total = total + taps[k : k + 1] * scratch[8 - back + k : 8 - back + k + length, :width]
    return (total / (1.0 + jnp.exp(-total))).astype(jnp.bfloat16)


def without_halo(
    x_ref, b_ref, dt_ref, bias_ref, alog_ref, tx_ref, tb_ref,
    message_ref, logs_out, delta_out, scratch, b_scratch, extra,
):
    length, width = x_ref.shape
    back = tx_ref.shape[0] - 1
    nothing = jnp.zeros((8, 128), jnp.bfloat16)
    b_act = conv_silu(nothing, b_ref[...], tb_ref[...], b_scratch)
    raw = dt_ref[...] + bias_ref[...].T
    grown = jnp.exp(-jnp.abs(raw))
    one_more = 1.0 + grown
    ratio = grown / jnp.where(one_more == 1.0, 1.0, one_more - 1.0)
    delta = jnp.maximum(raw, 0.0) + jnp.where(one_more == 1.0, grown, jnp.log(one_more) * ratio)
    rates = -jnp.exp(alog_ref[...].T) * delta
    until = (
        lax.broadcasted_iota(jnp.int32, (length, length), 0)
        <= lax.broadcasted_iota(jnp.int32, (length, length), 1)
    ).astype(jnp.bfloat16)
    logs = jnp.zeros(rates.shape, jnp.float32)
    for part in split3(rates):
        logs = logs + jnp.dot(part, until, preferred_element_type=jnp.float32)
    last = logs[:, length - 1 : length]
    logs_out[...] = logs
    delta_out[...] = delta
    scale = (jnp.exp(last - logs) * delta).T
    decay = [part.astype(jnp.float32) for part in split3(jnp.exp(last))]
    lane = lax.broadcasted_iota(jnp.int32, (length, 128), 1)
    late = lax.broadcasted_iota(jnp.int32, (length, 128), 0) >= back
    extra[...] = jnp.zeros(extra.shape, jnp.float32)
    for p in range(width // 128):
        here = slice(128 * p, 128 * p + 128)
        x_act = conv_silu(nothing, x_ref[:, here], tx_ref[:, here], scratch)
        factor = jnp.where(lane < 64, scale[:, 2 * p : 2 * p + 1], scale[:, 2 * p + 1 : 2 * p + 2])
        scaled = jnp.where(late, factor * x_act.astype(jnp.float32), 0.0).astype(jnp.bfloat16)
        update = lax.dot_general(
            scaled, b_act, (((0,), (0,)), ((), ())), preferred_element_type=jnp.float32
        )
        message_ref[p, 0:128, :] = update.astype(jnp.bfloat16)
        for k in range(6):
            h = 2 * p + k % 2
            extra[k : k + 1, :] = jnp.broadcast_to(decay[k // 2][h : h + 1, :], (1, 128))
        extra[6:9, :] = scratch[8:11, :]
        extra[9:12, :] = scratch[5 + length : 8 + length, :]
        extra[12:15, :] = b_scratch[8:11, :]
        extra[15:18, :] = b_scratch[5 + length : 8 + length, :]
        for k, part in enumerate(split3(factor[0:8])):
            extra[18 + 3 * k : 21 + 3 * k, :] = part.astype(jnp.float32)[0:3]
        message_ref[p, 128 : 128 + EXTRA, :] = extra[...].astype(jnp.bfloat16)


def all_rows(
    tail_ref, x_ref, b_ref, c_ref, tx_ref, tb_ref, tc_ref, x_out, b_out, c_out, scratch
):
    width, state = x_ref.shape[1], b_ref.shape[1]
    for p in range(width // 128):
        here = slice(128 * p, 128 * p + 128)
        x_out[:, here] = conv_silu(tail_ref[8:16, here], x_ref[:, here], tx_ref[:, here], scratch)
    b_out[...] = conv_silu(
        tail_ref[8:16, width : width + state], b_ref[...], tb_ref[...], scratch
    )
    c_out[...] = conv_silu(tail_ref[8:16, width + state :], c_ref[...], tc_ref[...], scratch)


def widen(decay):
    return jnp.repeat(decay, 64, axis=-2)


def own_taps(first, taps):
    return sum(
        jnp.pad(taps[k] * first[..., : k, :], [(0, 0)] * (first.ndim - 2) + [(3 - k, 0), (0, 0)])
        for k in range(1, 4)
    )


def tail_taps(tail, taps):
    return sum(
        jnp.pad(taps[k] * tail[..., k:, :], [(0, 0)] * (tail.ndim - 2) + [(0, k), (0, 0)])
        for k in range(3)
    )


def near_groups():
    count = lax.axis_size("ctx")
    return [list(range(g * NEAR, (g + 1) * NEAR)) for g in range(count // NEAR)]


def first_update(total_x, total_b, scale):
    scaled = scale * jax.nn.silu(total_x).astype(jnp.bfloat16).astype(jnp.float32)
    return jnp.einsum(
        "...tc,...tn->...cn",
        scaled.astype(jnp.bfloat16),
        jax.nn.silu(total_b).astype(jnp.bfloat16),
        preferred_element_type=jnp.float32,
    )


def entering_states(message, conv_x, conv_b, late, make_local):
    f32, bf16 = jnp.float32, jnp.bfloat16
    near = near_groups()
    place = lax.axis_index("ctx") % NEAR
    taps_x = lax.dynamic_slice_in_dim(conv_x, place * 128, 128, 1)
    taps_b = conv_b
    rest = message[:, 128:].astype(f32)
    part_decays = rest[:, 0:2] + rest[:, 2:4] + rest[:, 4:6]
    first_x, tail_x, first_b, tail_b = (rest[:, 6 + 3 * i : 9 + 3 * i] for i in range(4))
    scale = rest[:, 18:21] + rest[:, 21:24] + rest[:, 24:27]
    shifted = [jnp.pad(v[:-1], ((1, 0), (0, 0), (0, 0))) for v in (tail_x, tail_b)]
    firsts = first_update(
        own_taps(first_x, taps_x) + tail_taps(shifted[0], taps_x),
        own_taps(first_b, taps_b) + tail_taps(shifted[1], taps_b),
        scale,
    )
    parts = message[:, :128].astype(f32)
    parts = [parts[0], *(parts[k] + firsts[k] for k in range(1, NEAR))]
    inside, decays = [jnp.zeros((128, 128), f32)], [jnp.ones((2, 128), f32)]
    after = [jnp.zeros((2, 128), f32), jnp.ones((2, 128), f32)]
    for k in range(NEAR):
        inside.append(widen(part_decays[k]) * inside[-1] + parts[k])
        decays.append(decays[-1] * part_decays[k])
        if k:
            after.append(after[-1] * part_decays[k])
    base, decay = inside[NEAR], widen(decays[NEAR])
    block = message[NEAR - 1, 128 + 9 : 128 + 18]
    ends = jnp.pad(jnp.concatenate([block[0:3], block[6:9]], axis=0), ((0, 10), (0, 0)))
    known = (own_taps(first_x[0], taps_x), own_taps(first_b[0], taps_b), scale[0])

    def change(rows, own_x, own_b, scale):
        x_part, b_part = tail_taps(rows[0:3], taps_x), tail_taps(rows[3:6], taps_b)
        return first_update(own_x + x_part, own_b + b_part, scale)

    def send(value, pairs):
        pairs = [(i, i + NEAR * (t - g)) for g, t in pairs for i in near[g]]
        return lax.ppermute(value, "ctx", pairs)

    behind = widen(after[NEAR])
    total = base + behind * firsts[0]
    came = send(jnp.concatenate([total.astype(bf16), ends], axis=0), [(0, 1)]).astype(f32)
    entry, rows = came[:128], came[128:]
    base, known, ends = lax.optimization_barrier((base, known, ends))
    thirds = [
        lax.reduce_precision(v, 8, 7)
        for d in (decays[NEAR], after[NEAR])
        for v in (d, d - lax.reduce_precision(d, 8, 7))
    ]
    extra = (first_x[0], first_b[0], *(rest[0, 18 + 3 * i : 21 + 3 * i] for i in range(3)), *thirds)
    half = len(near) // 2
    for g in range(1, half):
        on = (decay * came[:128] + base + behind * change(came[128:], *known)).astype(bf16)
        sent = jnp.concatenate([on, ends], axis=0)
        if g == half - 2:
            sent, extra = lax.optimization_barrier((sent, extra))
        if g < half - 1:
            came = send(sent, [(g, g + 1)])
            if g == 1:
                base_low, late, came = lax.optimization_barrier((base.astype(bf16), late, came))
                local = make_local(late)
            came = came.astype(f32)
            entry, rows = entry + came[:128], rows + came[128:]
    extra = jnp.concatenate(extra, axis=0).astype(bf16)
    extra = jnp.pad(extra, ((0, 32 - extra.shape[0]), (0, 0)))
    even = jnp.concatenate([base_low, ends, extra], axis=0)
    groups = len(near)
    even = send(even, [(g, g + 1) for g in range(half, groups, 2)])
    far = jnp.zeros((144, 128), f32)
    for g in range(half - 1, groups - 1, 2):
        sent = jnp.concatenate([on, ends], axis=0)
        came = send(sent, [(g, g + 2)])
        if g == groups - 3:
            sent, came = lax.optimization_barrier((sent, came))
        if g == half - 1:
            even, came, local = lax.optimization_barrier((even, came, local))
            even = even.astype(f32)
            base_e, ends_e, extra = even[:128], even[128:144], even[144:]
            known_e = (
                own_taps(extra[0:3], taps_x),
                own_taps(extra[3:6], taps_b),
                extra[6:9] + extra[9:12] + extra[12:15],
            )
            decay_e = widen(extra[15:17] + extra[17:19])
            behind_e = widen(extra[19:21] + extra[21:23])
            rows = rows + ends_e
            odd = (decay * decay_e, decay * base_e + base + behind * change(ends_e, *known))
            odd = lax.optimization_barrier((*odd, decay * behind_e, decay_e, base_e, behind_e, known_e))
            step, own, first_e, decay_e, base_e, behind_e, known_e = odd
        came = came.astype(f32)
        beside = send(sent, [(g, g + 1)]).astype(f32)
        entry, rows, far = entry + beside[:128], rows + beside[128:], far + came
        on = (step * came[:128] + own + first_e * change(came[128:], *known_e)).astype(bf16)
    inside = jnp.stack(inside[:NEAR]) + widen(jnp.stack(after[:NEAR])) * (
        change(rows, *known)
    )
    decays = widen(jnp.stack(decays[:NEAR]))
    inside, decays, entry = lax.optimization_barrier((inside, decays, entry + base_e))
    before = entry + decay_e * far[:128] + behind_e * change(far[128:], *known_e)
    states = (inside + decays * before).astype(bf16)
    states = lax.all_to_all(states, "ctx", 0, 0, tiled=True, axis_index_groups=near)
    return states.reshape(NEAR * 128, 128), local


def halo(tails):
    count = lax.axis_size("ctx")
    return lax.ppermute(tails, "ctx", [(i, i + 1) for i in range(count - 1)])


def shards(
    x_in, z_in, b_in, c_in, dt_raw, dt_bias, a_log, d_skip, conv_x, conv_b, conv_c, norm_gain
):
    length, width = x_in.shape
    heads = dt_raw.shape[1]
    head_size = width // heads
    state = b_in.shape[1]
    count = lax.axis_size("ctx")
    whole = width + 2 * state
    f32, bf16 = jnp.float32, jnp.bfloat16
    shape = jax.ShapeDtypeStruct
    message, logs, delta = pl.pallas_call(
        without_halo,
        out_shape=[
            shape((width // 128, 128 + EXTRA, state), bf16),
            shape((heads, length), f32),
            shape((heads, length), f32),
        ],
        scratch_shapes=[
            pltpu.VMEM((8 + length, 128), f32),
            pltpu.VMEM((8 + length, 128), f32),
            pltpu.VMEM((EXTRA, 128), f32),
        ],
        compiler_params=pltpu.CompilerParams(vmem_limit_bytes=HIGH),
        name="without_halo",
    )(x_in, b_in, dt_raw.T, dt_bias[None], a_log[None], conv_x, conv_b)
    late_x, late_b, late_c, _ = lax.optimization_barrier((x_in, b_in, c_in, message))
    end = length // 16 - 1
    tails = pl.pallas_call(
        pack_tails,
        grid=(1,),
        in_specs=[pl.BlockSpec((16, v), lambda i: (end, 0)) for v in (width, state, state)],
        out_specs=pl.BlockSpec((16, whole), lambda i: (0, 0)),
        out_shape=shape((16, whole), bf16),
        name="pack_tails",
    )(late_x, late_b, late_c)
    tails = halo(tails)
    x_act, b_act, c_act = pl.pallas_call(
        all_rows,
        out_shape=[shape((length, v), bf16) for v in (width, state, state)],
        scratch_shapes=[pltpu.VMEM((8 + length, 128), f32)],
        compiler_params=pltpu.CompilerParams(vmem_limit_bytes=LOW),
        name="all_rows",
    )(tails, late_x, late_b, late_c, conv_x, conv_b, conv_c)
    message = lax.all_to_all(message, "ctx", 0, 0, tiled=True, axis_index_groups=near_groups())
    message, x_act, b_act, c_act = lax.optimization_barrier((message, x_act, b_act, c_act))
    def make_local(delta):
        lower = jnp.triu(jnp.ones((SPAN, SPAN), dtype=bool))
        x_heads = x_act.T.reshape(heads, head_size, length)
        scores = jnp.dot(b_act, c_act.T, preferred_element_type=f32)
        decay = jnp.exp(jnp.where(lower[None], logs[:, None, :] - logs[:, :, None], -jnp.inf))
        weights = (scores[None] * decay * delta[:, :, None]).astype(bf16)
        inner = jnp.einsum("hst,hps->hpt", weights, x_heads, preferred_element_type=f32)
        inner = inner + d_skip[:, None, None] * x_heads.astype(f32)
        gate = jax.nn.silu(z_in.astype(f32)).T
        return inner, gate, gate * norm_gain[:, None], jnp.exp(logs)

    state_low, local = entering_states(message, conv_x, conv_b, delta, make_local)
    inner, gate, gain, grown = local
    outer = jnp.dot(state_low, c_act.T, preferred_element_type=f32)
    y_val = inner + grown[:, None, :] * outer.reshape(heads, head_size, length)
    y_val = y_val.reshape(width, length)
    gated = y_val * gate
    meansq = jnp.mean(gated * gated, axis=0, keepdims=True)
    normed = (y_val * gain * lax.rsqrt(meansq + 1e-05)).astype(bf16)
    return lax.all_to_all(normed, "ctx", split_axis=0, concat_axis=1, tiled=True)


def solution(mesh):
    return jax.shard_map(
        shards,
        mesh=mesh,
        in_specs=(
            P("ctx", "tp"),
            P("ctx", "tp"),
            P("ctx", "tp"),
            P("ctx", "tp"),
            P("ctx", "tp"),
            P("tp"),
            P("tp"),
            P("tp"),
            P(None, "tp"),
            P(None, "tp"),
            P(None, "tp"),
            P("tp"),
        ),
        out_specs=P(("tp", "ctx"), None),
        check_vma=False,
    )
```

```python
import jax
import jax.numpy as jnp
from jax import lax
from jax.experimental import pallas as pl
from jax.experimental.pallas import tpu as pltpu
from jax.sharding import PartitionSpec as P

SPAN = 128
NEAR = 8
EXTRA = 32
LOW = 20 << 20
HIGH = 56 << 20


def split3(value):
    first = value.astype(jnp.bfloat16)
    rest = value - first.astype(jnp.float32)
    second = rest.astype(jnp.bfloat16)
    third = (rest - second.astype(jnp.float32)).astype(jnp.bfloat16)
    return [first, second, third]


def pack_tails(x_ref, b_ref, c_ref, out_ref):
    width, state = x_ref.shape[1], b_ref.shape[1]
    out_ref[:, :width] = x_ref[...]
    out_ref[:, width : width + state] = b_ref[...]
    out_ref[:, width + state :] = c_ref[...]


def conv_silu(tail, rows, taps, scratch):
    length, width = rows.shape
    back = taps.shape[0] - 1
    scratch[0:8, :width] = tail.astype(jnp.float32)
    scratch[8 : 8 + length, :width] = rows.astype(jnp.float32)
    total = taps[0:1] * scratch[8 - back : 8 - back + length, :width]
    for k in range(1, back + 1):
        total = total + taps[k : k + 1] * scratch[8 - back + k : 8 - back + k + length, :width]
    return (total / (1.0 + jnp.exp(-total))).astype(jnp.bfloat16)


def without_halo(
    x_ref, b_ref, dt_ref, bias_ref, alog_ref, tx_ref, tb_ref,
    message_ref, logs_out, delta_out, scratch, b_scratch, extra,
):
    length, width = x_ref.shape
    back = tx_ref.shape[0] - 1
    nothing = jnp.zeros((8, 128), jnp.bfloat16)
    b_act = conv_silu(nothing, b_ref[...], tb_ref[...], b_scratch)
    raw = dt_ref[...] + bias_ref[...].T
    grown = jnp.exp(-jnp.abs(raw))
    one_more = 1.0 + grown
    ratio = grown / jnp.where(one_more == 1.0, 1.0, one_more - 1.0)
    delta = jnp.maximum(raw, 0.0) + jnp.where(one_more == 1.0, grown, jnp.log(one_more) * ratio)
    rates = -jnp.exp(alog_ref[...].T) * delta
    until = (
        lax.broadcasted_iota(jnp.int32, (length, length), 0)
        <= lax.broadcasted_iota(jnp.int32, (length, length), 1)
    ).astype(jnp.bfloat16)
    logs = jnp.zeros(rates.shape, jnp.float32)
    for part in split3(rates):
        logs = logs + jnp.dot(part, until, preferred_element_type=jnp.float32)
    last = logs[:, length - 1 : length]
    logs_out[...] = logs
    delta_out[...] = delta
    scale = (jnp.exp(last - logs) * delta).T
    decay = [part.astype(jnp.float32) for part in split3(jnp.exp(last))]
    lane = lax.broadcasted_iota(jnp.int32, (length, 128), 1)
    late = lax.broadcasted_iota(jnp.int32, (length, 128), 0) >= back
    extra[...] = jnp.zeros(extra.shape, jnp.float32)
    for p in range(width // 128):
        here = slice(128 * p, 128 * p + 128)
        x_act = conv_silu(nothing, x_ref[:, here], tx_ref[:, here], scratch)
        factor = jnp.where(lane < 64, scale[:, 2 * p : 2 * p + 1], scale[:, 2 * p + 1 : 2 * p + 2])
        scaled = jnp.where(late, factor * x_act.astype(jnp.float32), 0.0).astype(jnp.bfloat16)
        update = lax.dot_general(
            scaled, b_act, (((0,), (0,)), ((), ())), preferred_element_type=jnp.float32
        )
        message_ref[p, 0:128, :] = update.astype(jnp.bfloat16)
        for k in range(6):
            h = 2 * p + k % 2
            extra[k : k + 1, :] = jnp.broadcast_to(decay[k // 2][h : h + 1, :], (1, 128))
        extra[6:9, :] = scratch[8:11, :]
        extra[9:12, :] = scratch[5 + length : 8 + length, :]
        extra[12:15, :] = b_scratch[8:11, :]
        extra[15:18, :] = b_scratch[5 + length : 8 + length, :]
        for k, part in enumerate(split3(factor[0:8])):
            extra[18 + 3 * k : 21 + 3 * k, :] = part.astype(jnp.float32)[0:3]
        message_ref[p, 128 : 128 + EXTRA, :] = extra[...].astype(jnp.bfloat16)


def all_rows(
    tail_ref, x_ref, b_ref, c_ref, tx_ref, tb_ref, tc_ref, x_out, b_out, c_out, scratch
):
    width, state = x_ref.shape[1], b_ref.shape[1]
    for p in range(width // 128):
        here = slice(128 * p, 128 * p + 128)
        x_out[:, here] = conv_silu(tail_ref[8:16, here], x_ref[:, here], tx_ref[:, here], scratch)
    b_out[...] = conv_silu(
        tail_ref[8:16, width : width + state], b_ref[...], tb_ref[...], scratch
    )
    c_out[...] = conv_silu(tail_ref[8:16, width + state :], c_ref[...], tc_ref[...], scratch)


def widen(decay):
    return jnp.repeat(decay, 64, axis=-2)


def own_taps(first, taps):
    return sum(
        jnp.pad(taps[k] * first[..., : k, :], [(0, 0)] * (first.ndim - 2) + [(3 - k, 0), (0, 0)])
        for k in range(1, 4)
    )


def tail_taps(tail, taps):
    return sum(
        jnp.pad(taps[k] * tail[..., k:, :], [(0, 0)] * (tail.ndim - 2) + [(0, k), (0, 0)])
        for k in range(3)
    )


def near_groups():
    count = lax.axis_size("ctx")
    return [list(range(g * NEAR, (g + 1) * NEAR)) for g in range(count // NEAR)]


def first_update(total_x, total_b, scale):
    scaled = scale * jax.nn.silu(total_x).astype(jnp.bfloat16).astype(jnp.float32)
    return jnp.einsum(
        "...tc,...tn->...cn",
        scaled.astype(jnp.bfloat16),
        jax.nn.silu(total_b).astype(jnp.bfloat16),
        preferred_element_type=jnp.float32,
    )


def entering_states(message, conv_x, conv_b, late, make_local):
    f32, bf16 = jnp.float32, jnp.bfloat16
    near = near_groups()
    place = lax.axis_index("ctx") % NEAR
    taps_x = lax.dynamic_slice_in_dim(conv_x, place * 128, 128, 1)
    taps_b = conv_b
    rest = message[:, 128:].astype(f32)
    part_decays = rest[:, 0:2] + rest[:, 2:4] + rest[:, 4:6]
    first_x, tail_x, first_b, tail_b = (rest[:, 6 + 3 * i : 9 + 3 * i] for i in range(4))
    scale = rest[:, 18:21] + rest[:, 21:24] + rest[:, 24:27]
    shifted = [jnp.pad(v[:-1], ((1, 0), (0, 0), (0, 0))) for v in (tail_x, tail_b)]
    firsts = first_update(
        own_taps(first_x, taps_x) + tail_taps(shifted[0], taps_x),
        own_taps(first_b, taps_b) + tail_taps(shifted[1], taps_b),
        scale,
    )
    parts = message[:, :128].astype(f32)
    parts = [parts[0], *(parts[k] + firsts[k] for k in range(1, NEAR))]
    inside, decays = [jnp.zeros((128, 128), f32)], [jnp.ones((2, 128), f32)]
    after = [jnp.zeros((2, 128), f32), jnp.ones((2, 128), f32)]
    for k in range(NEAR):
        inside.append(widen(part_decays[k]) * inside[-1] + parts[k])
        decays.append(decays[-1] * part_decays[k])
        if k:
            after.append(after[-1] * part_decays[k])
    base, decay = inside[NEAR], widen(decays[NEAR])
    block = message[NEAR - 1, 128 + 9 : 128 + 18]
    ends = jnp.pad(jnp.concatenate([block[0:3], block[6:9]], axis=0), ((0, 10), (0, 0)))
    known = (own_taps(first_x[0], taps_x), own_taps(first_b[0], taps_b), scale[0])

    def change(rows, own_x, own_b, scale):
        x_part, b_part = tail_taps(rows[0:3], taps_x), tail_taps(rows[3:6], taps_b)
        return first_update(own_x + x_part, own_b + b_part, scale)

    def send(value, pairs):
        pairs = [(i, i + NEAR * (t - g)) for g, t in pairs for i in near[g]]
        return lax.ppermute(value, "ctx", pairs)

    behind = widen(after[NEAR])
    total = base + behind * firsts[0]
    came = send(jnp.concatenate([total.astype(bf16), ends], axis=0), [(0, 1)]).astype(f32)
    entry, rows = came[:128], came[128:]
    base, known, ends = lax.optimization_barrier((base, known, ends))
    thirds = [
        lax.reduce_precision(v, 8, 7)
        for d in (decays[NEAR], after[NEAR])
        for v in (d, d - lax.reduce_precision(d, 8, 7))
    ]
    extra = (first_x[0], first_b[0], *(rest[0, 18 + 3 * i : 21 + 3 * i] for i in range(3)), *thirds)
    half = len(near) // 2
    for g in range(1, half):
        on = (decay * came[:128] + base + behind * change(came[128:], *known)).astype(bf16)
        sent = jnp.concatenate([on, ends], axis=0)
        if g == half - 2:
            sent, extra, late = lax.optimization_barrier((sent, extra, late))
            local = make_local(*late)
        if g < half - 1:
            came = send(sent, [(g, g + 1)])
            if g == 1:
                base_low, came = lax.optimization_barrier((base.astype(bf16), came))
            came = came.astype(f32)
            entry, rows = entry + came[:128], rows + came[128:]
    extra = jnp.concatenate(extra, axis=0).astype(bf16)
    extra = jnp.pad(extra, ((0, 32 - extra.shape[0]), (0, 0)))
    even = jnp.concatenate([base_low, ends, extra], axis=0)
    groups = len(near)
    even = send(even, [(g, g + 1) for g in range(half, groups, 2)])
    far = jnp.zeros((144, 128), f32)
    for g in range(half - 1, groups - 1, 2):
        sent = jnp.concatenate([on, ends], axis=0)
        came = send(sent, [(g, g + 2)])
        if g == groups - 3:
            sent, came = lax.optimization_barrier((sent, came))
        if g == half - 1:
            even, came, local = lax.optimization_barrier((even, came, local))
            even = even.astype(f32)
            base_e, ends_e, extra = even[:128], even[128:144], even[144:]
            known_e = (
                own_taps(extra[0:3], taps_x),
                own_taps(extra[3:6], taps_b),
                extra[6:9] + extra[9:12] + extra[12:15],
            )
            decay_e = widen(extra[15:17] + extra[17:19])
            behind_e = widen(extra[19:21] + extra[21:23])
            rows = rows + ends_e
            odd = (decay * decay_e, decay * base_e + base + behind * change(ends_e, *known))
            odd = lax.optimization_barrier((*odd, decay * behind_e, decay_e, base_e, behind_e, known_e))
            step, own, first_e, decay_e, base_e, behind_e, known_e = odd
        came = came.astype(f32)
        beside = send(sent, [(g, g + 1)]).astype(f32)
        entry, rows, far = entry + beside[:128], rows + beside[128:], far + came
        on = (step * came[:128] + own + first_e * change(came[128:], *known_e)).astype(bf16)
    inside = jnp.stack(inside[:NEAR]) + widen(jnp.stack(after[:NEAR])) * (
        change(rows, *known)
    )
    decays = widen(jnp.stack(decays[:NEAR]))
    inside, decays, entry = lax.optimization_barrier((inside, decays, entry + base_e))
    before = entry + decay_e * far[:128] + behind_e * change(far[128:], *known_e)
    states = (inside + decays * before).astype(bf16)
    states = lax.all_to_all(states, "ctx", 0, 0, tiled=True, axis_index_groups=near)
    return states.reshape(NEAR * 128, 128), local


def halo(tails):
    count = lax.axis_size("ctx")
    return lax.ppermute(tails, "ctx", [(i, i + 1) for i in range(count - 1)])


def shards(
    x_in, z_in, b_in, c_in, dt_raw, dt_bias, a_log, d_skip, conv_x, conv_b, conv_c, norm_gain
):
    length, width = x_in.shape
    heads = dt_raw.shape[1]
    head_size = width // heads
    state = b_in.shape[1]
    count = lax.axis_size("ctx")
    whole = width + 2 * state
    f32, bf16 = jnp.float32, jnp.bfloat16
    shape = jax.ShapeDtypeStruct
    message, logs, delta = pl.pallas_call(
        without_halo,
        out_shape=[
            shape((width // 128, 128 + EXTRA, state), bf16),
            shape((heads, length), f32),
            shape((heads, length), f32),
        ],
        scratch_shapes=[
            pltpu.VMEM((8 + length, 128), f32),
            pltpu.VMEM((8 + length, 128), f32),
            pltpu.VMEM((EXTRA, 128), f32),
        ],
        compiler_params=pltpu.CompilerParams(vmem_limit_bytes=HIGH),
        name="without_halo",
    )(x_in, b_in, dt_raw.T, dt_bias[None], a_log[None], conv_x, conv_b)
    late_x, late_b, late_c, _ = lax.optimization_barrier((x_in, b_in, c_in, message))
    end = length // 16 - 1
    tails = pl.pallas_call(
        pack_tails,
        grid=(1,),
        in_specs=[pl.BlockSpec((16, v), lambda i: (end, 0)) for v in (width, state, state)],
        out_specs=pl.BlockSpec((16, whole), lambda i: (0, 0)),
        out_shape=shape((16, whole), bf16),
        name="pack_tails",
    )(late_x, late_b, late_c)
    tails = halo(tails)
    x_act, b_act, c_act = pl.pallas_call(
        all_rows,
        out_shape=[shape((length, v), bf16) for v in (width, state, state)],
        scratch_shapes=[pltpu.VMEM((8 + length, 128), f32)],
        compiler_params=pltpu.CompilerParams(vmem_limit_bytes=LOW),
        name="all_rows",
    )(tails, late_x, late_b, late_c, conv_x, conv_b, conv_c)
    message = lax.all_to_all(message, "ctx", 0, 0, tiled=True, axis_index_groups=near_groups())
    message, x_act, b_act, c_act = lax.optimization_barrier((message, x_act, b_act, c_act))
    def make_local(delta, x_act):
        lower = jnp.triu(jnp.ones((SPAN, SPAN), dtype=bool))
        x_heads = x_act.T.reshape(heads, head_size, length)
        scores = jnp.dot(b_act, c_act.T, preferred_element_type=f32)
        decay = jnp.exp(jnp.where(lower[None], logs[:, None, :] - logs[:, :, None], -jnp.inf))
        weights = (scores[None] * decay * delta[:, :, None]).astype(bf16)
        inner = jnp.einsum("hst,hps->hpt", weights, x_heads, preferred_element_type=f32)
        inner = inner + d_skip[:, None, None] * x_heads.astype(f32)
        gate = jax.nn.silu(z_in.astype(f32)).T
        return inner, gate, gate * norm_gain[:, None], jnp.exp(logs)

    state_low, local = entering_states(message, conv_x, conv_b, (delta, x_act), make_local)
    inner, gate, gain, grown = local
    outer = jnp.dot(state_low, c_act.T, preferred_element_type=f32)
    y_val = inner + grown[:, None, :] * outer.reshape(heads, head_size, length)
    y_val = y_val.reshape(width, length)
    gated = y_val * gate
    meansq = jnp.mean(gated * gated, axis=0, keepdims=True)
    normed = (y_val * gain * lax.rsqrt(meansq + 1e-05)).astype(bf16)
    return lax.all_to_all(normed, "ctx", split_axis=0, concat_axis=1, tiled=True)


def solution(mesh):
    return jax.shard_map(
        shards,
        mesh=mesh,
        in_specs=(
            P("ctx", "tp"),
            P("ctx", "tp"),
            P("ctx", "tp"),
            P("ctx", "tp"),
            P("ctx", "tp"),
            P("tp"),
            P("tp"),
            P("tp"),
            P(None, "tp"),
            P(None, "tp"),
            P(None, "tp"),
            P("tp"),
        ),
        out_specs=P(("tp", "ctx"), None),
        check_vma=False,
    )
```

```python
import jax
import jax.numpy as jnp
from jax import lax
from jax.experimental import pallas as pl
from jax.experimental.pallas import tpu as pltpu
from jax.sharding import PartitionSpec as P

SPAN = 128
NEAR = 8
EXTRA = 32
LOW = 20 << 20
HIGH = 56 << 20


def split3(value):
    first = value.astype(jnp.bfloat16)
    rest = value - first.astype(jnp.float32)
    second = rest.astype(jnp.bfloat16)
    third = (rest - second.astype(jnp.float32)).astype(jnp.bfloat16)
    return [first, second, third]


def pack_tails(x_ref, b_ref, c_ref, out_ref):
    width, state = x_ref.shape[1], b_ref.shape[1]
    out_ref[:, :width] = x_ref[...]
    out_ref[:, width : width + state] = b_ref[...]
    out_ref[:, width + state :] = c_ref[...]


def conv_silu(tail, rows, taps, scratch):
    length, width = rows.shape
    back = taps.shape[0] - 1
    scratch[0:8, :width] = tail.astype(jnp.float32)
    scratch[8 : 8 + length, :width] = rows.astype(jnp.float32)
    total = taps[0:1] * scratch[8 - back : 8 - back + length, :width]
    for k in range(1, back + 1):
        total = total + taps[k : k + 1] * scratch[8 - back + k : 8 - back + k + length, :width]
    return (total / (1.0 + jnp.exp(-total))).astype(jnp.bfloat16)


def without_halo(
    x_ref, b_ref, dt_ref, bias_ref, alog_ref, tx_ref, tb_ref,
    message_ref, logs_out, delta_out, scratch, b_scratch, extra,
):
    length, width = x_ref.shape
    back = tx_ref.shape[0] - 1
    nothing = jnp.zeros((8, 128), jnp.bfloat16)
    b_act = conv_silu(nothing, b_ref[...], tb_ref[...], b_scratch)
    raw = dt_ref[...] + bias_ref[...].T
    grown = jnp.exp(-jnp.abs(raw))
    one_more = 1.0 + grown
    ratio = grown / jnp.where(one_more == 1.0, 1.0, one_more - 1.0)
    delta = jnp.maximum(raw, 0.0) + jnp.where(one_more == 1.0, grown, jnp.log(one_more) * ratio)
    rates = -jnp.exp(alog_ref[...].T) * delta
    until = (
        lax.broadcasted_iota(jnp.int32, (length, length), 0)
        <= lax.broadcasted_iota(jnp.int32, (length, length), 1)
    ).astype(jnp.bfloat16)
    logs = jnp.zeros(rates.shape, jnp.float32)
    for part in split3(rates):
        logs = logs + jnp.dot(part, until, preferred_element_type=jnp.float32)
    last = logs[:, length - 1 : length]
    logs_out[...] = logs
    delta_out[...] = delta
    scale = (jnp.exp(last - logs) * delta).T
    decay = [part.astype(jnp.float32) for part in split3(jnp.exp(last))]
    lane = lax.broadcasted_iota(jnp.int32, (length, 128), 1)
    late = lax.broadcasted_iota(jnp.int32, (length, 128), 0) >= back
    extra[...] = jnp.zeros(extra.shape, jnp.float32)
    extra[12:15, :] = b_scratch[8:11, :]
    extra[15:18, :] = b_scratch[5 + length : 8 + length, :]
    for p in range(width // 128):
        here = slice(128 * p, 128 * p + 128)
        x_act = conv_silu(nothing, x_ref[:, here], tx_ref[:, here], scratch)
        factor = jnp.where(lane < 64, scale[:, 2 * p : 2 * p + 1], scale[:, 2 * p + 1 : 2 * p + 2])
        scaled = jnp.where(late, factor * x_act.astype(jnp.float32), 0.0).astype(jnp.bfloat16)
        update = lax.dot_general(
            scaled, b_act, (((0,), (0,)), ((), ())), preferred_element_type=jnp.float32
        )
        message_ref[p, 0:128, :] = update.astype(jnp.bfloat16)
        for k in range(6):
            h = 2 * p + k % 2
            extra[k : k + 1, :] = jnp.broadcast_to(decay[k // 2][h : h + 1, :], (1, 128))
        extra[6:9, :] = scratch[8:11, :]
        extra[9:12, :] = scratch[5 + length : 8 + length, :]
        for k, part in enumerate(split3(factor[0:8])):
            extra[18 + 3 * k : 21 + 3 * k, :] = part.astype(jnp.float32)[0:3]
        message_ref[p, 128 : 128 + EXTRA, :] = extra[...].astype(jnp.bfloat16)


def all_rows(
    tail_ref, x_ref, b_ref, c_ref, tx_ref, tb_ref, tc_ref, x_out, b_out, c_out, scratch
):
    width, state = x_ref.shape[1], b_ref.shape[1]
    for p in range(width // 128):
        here = slice(128 * p, 128 * p + 128)
        x_out[:, here] = conv_silu(tail_ref[8:16, here], x_ref[:, here], tx_ref[:, here], scratch)
    b_out[...] = conv_silu(
        tail_ref[8:16, width : width + state], b_ref[...], tb_ref[...], scratch
    )
    c_out[...] = conv_silu(tail_ref[8:16, width + state :], c_ref[...], tc_ref[...], scratch)


def widen(decay):
    return jnp.repeat(decay, 64, axis=-2)


def own_taps(first, taps):
    return sum(
        jnp.pad(taps[k] * first[..., : k, :], [(0, 0)] * (first.ndim - 2) + [(3 - k, 0), (0, 0)])
        for k in range(1, 4)
    )


def tail_taps(tail, taps):
    return sum(
        jnp.pad(taps[k] * tail[..., k:, :], [(0, 0)] * (tail.ndim - 2) + [(0, k), (0, 0)])
        for k in range(3)
    )


def near_groups():
    count = lax.axis_size("ctx")
    return [list(range(g * NEAR, (g + 1) * NEAR)) for g in range(count // NEAR)]


def first_update(total_x, total_b, scale):
    scaled = scale * jax.nn.silu(total_x).astype(jnp.bfloat16).astype(jnp.float32)
    return jnp.einsum(
        "...tc,...tn->...cn",
        scaled.astype(jnp.bfloat16),
        jax.nn.silu(total_b).astype(jnp.bfloat16),
        preferred_element_type=jnp.float32,
    )


def entering_states(message, conv_x, conv_b, late, make_local):
    f32, bf16 = jnp.float32, jnp.bfloat16
    near = near_groups()
    place = lax.axis_index("ctx") % NEAR
    taps_x = lax.dynamic_slice_in_dim(conv_x, place * 128, 128, 1)
    taps_b = conv_b
    rest = message[:, 128:].astype(f32)
    part_decays = rest[:, 0:2] + rest[:, 2:4] + rest[:, 4:6]
    first_x, tail_x, first_b, tail_b = (rest[:, 6 + 3 * i : 9 + 3 * i] for i in range(4))
    scale = rest[:, 18:21] + rest[:, 21:24] + rest[:, 24:27]
    shifted = [jnp.pad(v[:-1], ((1, 0), (0, 0), (0, 0))) for v in (tail_x, tail_b)]
    firsts = first_update(
        own_taps(first_x, taps_x) + tail_taps(shifted[0], taps_x),
        own_taps(first_b, taps_b) + tail_taps(shifted[1], taps_b),
        scale,
    )
    parts = message[:, :128].astype(f32)
    parts = [parts[0], *(parts[k] + firsts[k] for k in range(1, NEAR))]
    inside, decays = [jnp.zeros((128, 128), f32)], [jnp.ones((2, 128), f32)]
    after = [jnp.zeros((2, 128), f32), jnp.ones((2, 128), f32)]
    for k in range(NEAR):
        inside.append(widen(part_decays[k]) * inside[-1] + parts[k])
        decays.append(decays[-1] * part_decays[k])
        if k:
            after.append(after[-1] * part_decays[k])
    base, decay = inside[NEAR], widen(decays[NEAR])
    block = message[NEAR - 1, 128 + 9 : 128 + 18]
    ends = jnp.pad(jnp.concatenate([block[0:3], block[6:9]], axis=0), ((0, 10), (0, 0)))
    known = (own_taps(first_x[0], taps_x), own_taps(first_b[0], taps_b), scale[0])

    def change(rows, own_x, own_b, scale):
        x_part, b_part = tail_taps(rows[0:3], taps_x), tail_taps(rows[3:6], taps_b)
        return first_update(own_x + x_part, own_b + b_part, scale)

    def send(value, pairs):
        pairs = [(i, i + NEAR * (t - g)) for g, t in pairs for i in near[g]]
        return lax.ppermute(value, "ctx", pairs)

    behind = widen(after[NEAR])
    total = base + behind * firsts[0]
    came = send(jnp.concatenate([total.astype(bf16), ends], axis=0), [(0, 1)]).astype(f32)
    entry, rows = came[:128], came[128:]
    base, known, ends = lax.optimization_barrier((base, known, ends))
    thirds = [
        lax.reduce_precision(v, 8, 7)
        for d in (decays[NEAR], after[NEAR])
        for v in (d, d - lax.reduce_precision(d, 8, 7))
    ]
    extra = (first_x[0], first_b[0], *(rest[0, 18 + 3 * i : 21 + 3 * i] for i in range(3)), *thirds)
    half = len(near) // 2
    for g in range(1, half):
        on = (decay * came[:128] + base + behind * change(came[128:], *known)).astype(bf16)
        sent = jnp.concatenate([on, ends], axis=0)
        if g == half - 2:
            sent, extra, late = lax.optimization_barrier((sent, extra, late))
            local = make_local(*late)
        if g < half - 1:
            came = send(sent, [(g, g + 1)])
            if g == 1:
                base_low, came = lax.optimization_barrier((base.astype(bf16), came))
            came = came.astype(f32)
            entry, rows = entry + came[:128], rows + came[128:]
    extra = jnp.concatenate(extra, axis=0).astype(bf16)
    extra = jnp.pad(extra, ((0, 32 - extra.shape[0]), (0, 0)))
    even = jnp.concatenate([base_low, ends, extra], axis=0)
    groups = len(near)
    even = send(even, [(g, g + 1) for g in range(half, groups, 2)])
    far = jnp.zeros((144, 128), f32)
    for g in range(half - 1, groups - 1, 2):
        sent = jnp.concatenate([on, ends], axis=0)
        came = send(sent, [(g, g + 2)])
        if g == groups - 3:
            sent, came = lax.optimization_barrier((sent, came))
        if g == half - 1:
            even, came, local = lax.optimization_barrier((even, came, local))
            even = even.astype(f32)
            base_e, ends_e, extra = even[:128], even[128:144], even[144:]
            known_e = (
                own_taps(extra[0:3], taps_x),
                own_taps(extra[3:6], taps_b),
                extra[6:9] + extra[9:12] + extra[12:15],
            )
            decay_e = widen(extra[15:17] + extra[17:19])
            behind_e = widen(extra[19:21] + extra[21:23])
            rows = rows + ends_e
            odd = (decay * decay_e, decay * base_e + base + behind * change(ends_e, *known))
            odd = lax.optimization_barrier((*odd, decay * behind_e, decay_e, base_e, behind_e, known_e))
            step, own, first_e, decay_e, base_e, behind_e, known_e = odd
        came = came.astype(f32)
        beside = send(sent, [(g, g + 1)]).astype(f32)
        entry, rows, far = entry + beside[:128], rows + beside[128:], far + came
        on = (step * came[:128] + own + first_e * change(came[128:], *known_e)).astype(bf16)
    inside = jnp.stack(inside[:NEAR]) + widen(jnp.stack(after[:NEAR])) * (
        change(rows, *known)
    )
    decays = widen(jnp.stack(decays[:NEAR]))
    inside, decays, entry = lax.optimization_barrier((inside, decays, entry + base_e))
    before = entry + decay_e * far[:128] + behind_e * change(far[128:], *known_e)
    states = (inside + decays * before).astype(bf16)
    states = lax.all_to_all(states, "ctx", 0, 0, tiled=True, axis_index_groups=near)
    return states.reshape(NEAR * 128, 128), local


def halo(tails):
    count = lax.axis_size("ctx")
    return lax.ppermute(tails, "ctx", [(i, i + 1) for i in range(count - 1)])


def shards(
    x_in, z_in, b_in, c_in, dt_raw, dt_bias, a_log, d_skip, conv_x, conv_b, conv_c, norm_gain
):
    length, width = x_in.shape
    heads = dt_raw.shape[1]
    head_size = width // heads
    state = b_in.shape[1]
    count = lax.axis_size("ctx")
    whole = width + 2 * state
    f32, bf16 = jnp.float32, jnp.bfloat16
    shape = jax.ShapeDtypeStruct
    message, logs, delta = pl.pallas_call(
        without_halo,
        out_shape=[
            shape((width // 128, 128 + EXTRA, state), bf16),
            shape((heads, length), f32),
            shape((heads, length), f32),
        ],
        scratch_shapes=[
            pltpu.VMEM((8 + length, 128), f32),
            pltpu.VMEM((8 + length, 128), f32),
            pltpu.VMEM((EXTRA, 128), f32),
        ],
        compiler_params=pltpu.CompilerParams(vmem_limit_bytes=HIGH),
        name="without_halo",
    )(x_in, b_in, dt_raw.T, dt_bias[None], a_log[None], conv_x, conv_b)
    late_x, late_b, late_c, _ = lax.optimization_barrier((x_in, b_in, c_in, message))
    end = length // 16 - 1
    tails = pl.pallas_call(
        pack_tails,
        grid=(1,),
        in_specs=[pl.BlockSpec((16, v), lambda i: (end, 0)) for v in (width, state, state)],
        out_specs=pl.BlockSpec((16, whole), lambda i: (0, 0)),
        out_shape=shape((16, whole), bf16),
        name="pack_tails",
    )(late_x, late_b, late_c)
    tails = halo(tails)
    x_act, b_act, c_act = pl.pallas_call(
        all_rows,
        out_shape=[shape((length, v), bf16) for v in (width, state, state)],
        scratch_shapes=[pltpu.VMEM((8 + length, 128), f32)],
        compiler_params=pltpu.CompilerParams(vmem_limit_bytes=LOW),
        name="all_rows",
    )(tails, late_x, late_b, late_c, conv_x, conv_b, conv_c)
    message = lax.all_to_all(message, "ctx", 0, 0, tiled=True, axis_index_groups=near_groups())
    message, x_act, b_act, c_act = lax.optimization_barrier((message, x_act, b_act, c_act))
    def make_local(delta, x_act):
        lower = jnp.triu(jnp.ones((SPAN, SPAN), dtype=bool))
        x_heads = x_act.T.reshape(heads, head_size, length)
        scores = jnp.dot(b_act, c_act.T, preferred_element_type=f32)
        decay = jnp.exp(jnp.where(lower[None], logs[:, None, :] - logs[:, :, None], -jnp.inf))
        weights = (scores[None] * decay * delta[:, :, None]).astype(bf16)
        inner = jnp.einsum("hst,hps->hpt", weights, x_heads, preferred_element_type=f32)
        inner = inner + d_skip[:, None, None] * x_heads.astype(f32)
        gate = jax.nn.silu(z_in.astype(f32)).T
        return inner, gate, gate * norm_gain[:, None], jnp.exp(logs)

    state_low, local = entering_states(message, conv_x, conv_b, (delta, x_act), make_local)
    inner, gate, gain, grown = local
    outer = jnp.dot(state_low, c_act.T, preferred_element_type=f32)
    y_val = inner + grown[:, None, :] * outer.reshape(heads, head_size, length)
    y_val = y_val.reshape(width, length)
    gated = y_val * gate
    meansq = jnp.mean(gated * gated, axis=0, keepdims=True)
    normed = (y_val * gain * lax.rsqrt(meansq + 1e-05)).astype(bf16)
    return lax.all_to_all(normed, "ctx", split_axis=0, concat_axis=1, tiled=True)


def solution(mesh):
    return jax.shard_map(
        shards,
        mesh=mesh,
        in_specs=(
            P("ctx", "tp"),
            P("ctx", "tp"),
            P("ctx", "tp"),
            P("ctx", "tp"),
            P("ctx", "tp"),
            P("tp"),
            P("tp"),
            P("tp"),
            P(None, "tp"),
            P(None, "tp"),
            P(None, "tp"),
            P("tp"),
        ),
        out_specs=P(("tp", "ctx"), None),
        check_vma=False,
    )
```
